32 devices in a mesh: tensor: 2 (over x), expert: 8 (over z, y), replica: 2 (over core).
Axes of the slice: x: 2, y: 2, z: 4, core: 2. Of those that a mesh axis runs over, the one named last changes fastest.
Arguments:
- tokens: bfloat16 [6304, 768], P(('expert', 'replica')), may hold values from -6 to 6
- gains: float32 [2, 2, 768], replicated, may hold values from 0.5 to 1.5
- attn_qkv: bfloat16 [2, 3, 768, 768], P(None, None, None, 'tensor'), may hold values from -0.21875 to 0.21875
- attn_out: bfloat16 [2, 768, 768], P(None, 'tensor'), may hold values from -3 to 3
- router: bfloat16 [2, 768, 8], replicated, may hold values from -0.15625 to 0.15625
- expert_in: bfloat16 [2, 8, 768, 3072], P(None, 'expert', None, 'tensor'), may hold values from -0.21875 to 0.21875
- expert_out: bfloat16 [2, 8, 3072, 768], P(None, 'expert', 'tensor'), may hold values from -1.75 to 1.75
- routes: int32 [2, 6304, 2], P(None, ('expert', 'replica')), may hold values from 0 to 7, all different within a row; in each aligned block of 394 rows (0 to 393, 394 to 787, ..., all dimensions but the last counted through in order) at most 128 rows name the same one
- cotangent: bfloat16 [6304, 768], P(('expert', 'replica')), may hold values from -6 to 6
Outputs:
- mixed_out: bfloat16 [6304, 768], P(('expert', 'replica'))
- grad_tokens: float32 [6304, 768], P(('expert', 'replica'))
- grad_gains: float32 [2, 2, 768], replicated
- grad_attn_qkv: float32 [2, 3, 768, 768], P(None, None, None, 'tensor')
- grad_attn_out: float32 [2, 768, 768], P(None, 'tensor')
- grad_router: float32 [2, 768, 8], replicated
- grad_expert_in: float32 [2, 8, 768, 3072], P(None, 'expert', 'replica', 'tensor')
- grad_expert_out: float32 [2, 8, 3072, 768], P(None, 'expert', 'tensor', 'replica')
The draws below stay inside these ranges and needn't reach their ends.
Inputs may be any that keep to these rules, and one draw needn't show every extreme that they name: In the tokens of one block of 394, no expert is named by more than 128 routes, and in every draw some expert by exactly 128; the two experts of a token differ.
All inputs are finite; a program needn't handle non-finite values.
Results may differ from the reference program's by a relative error of at most 0.02.
Values may be sent and summed in bfloat16 or wider, within the bound.
No kernel may reach another device: no remote copies, remote signals or barrier semaphores. Data moves between devices by JAX's collectives and lax.ppermute only.
A program may use at most 192 MiB of HBM per device.

```python
import math
from functools import partial
import jax
import jax.numpy as jnp
import numpy as np
from jax import lax

D = 768
HEADS = 12
HEAD_DIM = 64
FF = 3072
SEQ = 197
LAYERS = 2
EXPERTS = 8
GROUPS = 16
TOK_DEV = 394
IMAGES = 32
TOKENS = 6304
CAP = 128


def shard_levels(own_key, shape, pieces, least, top_value):
    level = 1.0
    for position, parts in pieces:
        heights = jax.random.uniform(jax.random.fold_in(jax.random.fold_in(own_key, 6), position), (parts,), jnp.float32, least / len(pieces), top_value / len(pieces))
        level = level * jnp.repeat(jnp.exp(heights), shape[position] // parts).reshape((-1,) + (1,) * (len(shape) - 1 - position))
    return level


def routed_block(stream_key, own, number, rows, count, top, bound, lean):
    ranking = jax.random.permutation(stream_key, count)
    packed, common = load_shares(count, rows * top, bound, lean, True), load_shares(count, rows * top, bound, lean, False)
    places = jnp.arange(count)

    def named(tallies, rotation):
        used = int((tallies > 0).sum())
        fixed = max(1, used // 4)
        moved = fixed + (places - fixed + rotation * (used - fixed)) % max(1, count - fixed)
        return jnp.zeros((count,), jnp.int32).at[ranking[jnp.where(places < fixed, places, moved)]].set(jnp.asarray(tallies, jnp.int32))

    tallies = jnp.where(number % 4 == 0, named(packed, number // 4), named(common, number - number // 4 - 1))
    mixed = jax.random.permutation(jax.random.fold_in(own, 3), count)
    donor, sink = mixed[0:count // 2 * 2:2], mixed[1:count // 2 * 2:2]
    room = jnp.minimum(tallies[donor] - 1, bound - tallies[sink]) // 2
    room = jnp.where((donor == ranking[0]) | (sink == ranking[0]) | (tallies[sink] == 0), 0, jnp.maximum(room, 0))
    moved = jax.random.randint(jax.random.fold_in(own, 4), (count // 2,), 0, 1 << 20) % (room + 1)
    tallies = tallies.at[donor].add(-moved).at[sink].add(moved)
    members = jnp.searchsorted(jnp.cumsum(tallies), jnp.arange(rows * top), side="right").astype(jnp.int32)
    table = members.reshape(top, rows).T
    table = table[jax.random.permutation(jax.random.fold_in(own, 1), rows)]
    rotation = jax.random.randint(jax.random.fold_in(own, 2), (rows, 1), 0, top)
    return jnp.take_along_axis(table, (jnp.arange(top)[None, :] + rotation) % top, axis=1)


def load_shares(number_of, total, most, skew, full):
    weights = [(1 << 20) // math.isqrt(standing ** skew) + 1 for standing in range(1, number_of + 1)]
    largest = most if full else min(most, max(-(-total // number_of), total * weights[0] // sum(weights)))
    least = 1 if total - largest >= number_of - 1 else 0
    given, surplus = [largest] + [least] * (number_of - 1), total - largest - least * (number_of - 1)
    while surplus > 0:
        candidates = [i for i in range(1, number_of) if given[i] < largest] or [i for i in range(1, number_of) if given[i] < most]
        mass, remaining = sum([weights[i] for i in candidates]), surplus
        for i in candidates:
            extra = min(most - given[i], max(1, remaining * weights[i] // mass), surplus)
            given[i] = given[i] + extra
            surplus = surplus - extra
    return np.array(given)


def bell_draw(key, dims, scale, reach, split=(), kind=jnp.bfloat16):
    loudness = shard_levels(key, dims, split, -0.22, 0.18) if split else 1.0
    result = jax.random.normal(key, dims, jnp.float32) * scale * loudness
    return jnp.minimum(jnp.maximum(result, -reach), reach).astype(kind)


def setup_inputs(seed: int = 0) -> dict:
    streams_of = jax.random.split(jax.random.key(seed), 10)
    tokens = bell_draw(streams_of[0], (TOKENS, D), 1.0, 6.0, ((0, 16),))
    gains = jnp.clip(1.0 + 0.1 * jax.random.normal(streams_of[1], (LAYERS, 2, D), jnp.float32), 0.5, 1.5)
    attn_qkv = bell_draw(streams_of[2], (LAYERS, 3, D, D), D ** -0.5, 0.21875, ((3, 2),))
    attn_out = bell_draw(streams_of[3], (LAYERS, D, D), (max(D // 192, 1)) ** -0.5, 3.0, ((1, 2),))
    router = bell_draw(streams_of[4], (LAYERS, D, EXPERTS), (2 * D) ** -0.5, 0.15625)
    expert_in = bell_draw(streams_of[5], (LAYERS, EXPERTS, D, FF), D ** -0.5, 0.21875, ((1, 8), (3, 2)))
    expert_out = bell_draw(streams_of[6], (LAYERS, EXPERTS, FF, D), (max(FF // 256, 1)) ** -0.5, 1.75, ((1, 8), (2, 2)))
    routes_keys = jax.random.split(jax.random.fold_in(streams_of[7], 1), LAYERS * TOKENS // TOK_DEV)
    routes_turns = jax.random.permutation(jax.random.fold_in(streams_of[7], 3), LAYERS * TOKENS // TOK_DEV)
    routes = jax.vmap(lambda own, number: routed_block(jax.random.fold_in(streams_of[7], 2), own, number, TOK_DEV, EXPERTS, 2, CAP, 1))(routes_keys, routes_turns).reshape((LAYERS, TOKENS, 2))
    cotangent = bell_draw(streams_of[8], (TOKENS, D), 1.0, 6.0, ((0, 16),))
    return dict(tokens=tokens, gains=gains, attn_qkv=attn_qkv, attn_out=attn_out, router=router, expert_in=expert_in, expert_out=expert_out, routes=routes, cotangent=cotangent)


HIGHEST = lax.Precision.HIGHEST
EPSILON = 1e-06

@jax.custom_vjp
def low(v):
    return lax.optimization_barrier(v.astype(jnp.bfloat16)).astype(jnp.float32)

@jax.custom_vjp
def low_back(v):
    return v

def low_keep(v):
    return (low(v), None)

def low_pass(kept, grad):
    return (grad,)

def back_keep(v):
    return (v, None)

def back_low(kept, grad):
    return (low(grad),)
low.defvjp(low_keep, low_pass)
low_back.defvjp(back_keep, back_low)

def layer_norm(stream, gain):
    center = lax.optimization_barrier(jnp.mean(stream, axis=-1, keepdims=True))
    shifted = stream - center
    spread = lax.optimization_barrier(jnp.mean(shifted * shifted, axis=-1, keepdims=True))
    return shifted * lax.rsqrt(spread + EPSILON) * gain

def slot_table(route_ids):
    blocks = route_ids.reshape(GROUPS, TOK_DEV, 2)
    labels = jnp.arange(EXPERTS, dtype=jnp.int32)
    route_hits = lax.optimization_barrier(jnp.sum((blocks[..., None] == labels).astype(jnp.int32), axis=2))
    before = jnp.cumsum(route_hits, axis=1) - route_hits
    slot_rank = jnp.take_along_axis(before, blocks, axis=2)
    offsets = jnp.arange(GROUPS, dtype=jnp.int32)[:, None, None] * CAP
    placed = blocks * (GROUPS * CAP) + offsets + slot_rank
    return placed.reshape(TOKENS, 2).astype(jnp.int32)

def forward(tokens, gains, attn_qkv, attn_out, router, expert_in, expert_out, routes, places):
    residual = tokens
    for layer_index in range(LAYERS):
        normed = low(layer_norm(residual, gains[layer_index, 0]))
        projected = low_back(low(jnp.einsum('td,cdf->ctf', normed, attn_qkv[layer_index], precision=HIGHEST)))
        head_view = projected.reshape(3, IMAGES, SEQ, HEADS, HEAD_DIM)
        scores = low_back(jnp.einsum('bqhe,bkhe->bhqk', head_view[0], head_view[1], precision=HIGHEST) * HEAD_DIM ** (-0.5))
        attn_probs = low(jax.nn.softmax(scores, axis=-1))
        mixed_rows = jnp.einsum('bhqk,bkhe->bqhe', attn_probs, head_view[2], precision=HIGHEST).reshape(TOKENS, D)
        mixed_rows = low_back(low(mixed_rows))
        residual = residual + low_back(jnp.dot(mixed_rows, attn_out[layer_index], precision=HIGHEST))
        moe_in = low(layer_norm(residual, gains[layer_index, 1]))
        gate_probs = jax.nn.softmax(low_back(jnp.dot(moe_in, router[layer_index], precision=HIGHEST)), axis=-1)
        picked = jnp.take_along_axis(gate_probs, routes[layer_index], axis=1)
        slot_rows = places[layer_index].reshape(-1)
        buffer_rows = jnp.zeros((EXPERTS * GROUPS * CAP, D), jnp.float32).at[slot_rows].set(jnp.repeat(moe_in, 2, axis=0))
        buffer_rows = buffer_rows.reshape(EXPERTS, GROUPS * CAP, D)
        pre_act = low_back(jnp.einsum('esd,edf->esf', buffer_rows, expert_in[layer_index], precision=HIGHEST))
        activation = low(jax.nn.gelu(pre_act))
        expert_rows = low_back(jnp.einsum('esf,efd->esd', activation, expert_out[layer_index], precision=HIGHEST)).reshape(-1, D)
        chosen = expert_rows[slot_rows].reshape(TOKENS, 2, D)
        residual = residual + lax.optimization_barrier(jnp.sum(picked[:, :, None] * chosen, axis=1))
    return residual

def reference(tokens, gains, attn_qkv, attn_out, router, expert_in, expert_out, routes, cotangent):
    places = jnp.stack([slot_table(routes[layer_index]) for layer_index in range(LAYERS)])
    float_args = [item.astype(jnp.float32) for item in (tokens, gains, attn_qkv, attn_out, router, expert_in, expert_out)]
    output, pullback = jax.vjp(partial(forward, routes=routes, places=places), *float_args)
    gradients = pullback(cotangent.astype(jnp.float32))
    return (output.astype(jnp.bfloat16), gradients[0], gradients[1], gradients[2], gradients[3], gradients[4], gradients[5], gradients[6])
```

```python
import functools

import jax
import jax.numpy as jnp
from jax import lax
from jax.experimental import pallas as pl
from jax.experimental.pallas import tpu as pltpu
from jax.sharding import PartitionSpec as P

HEAD_DIM = 64
SEQ = 197
PAD = 208
PAIR = 2 * HEAD_DIM
EPSILON = 1e-06
GELU_A = 0.7978845608028654
GELU_B = 0.044715
F32 = jnp.float32
BF16 = jnp.bfloat16
NT = (((1,), (1,)), ((), ()))
TN = (((0,), (0,)), ((), ()))


def mm(a, b):
    return jnp.dot(a, b, preferred_element_type=F32)


def mm_nt(a, b):
    return lax.dot_general(a, b, NT, preferred_element_type=F32)


def mm_tn(a, b):
    return lax.dot_general(a, b, TN, preferred_element_type=F32)


def normalize(stream):
    shifted = stream - jnp.mean(stream, axis=-1, keepdims=True)
    scale = lax.rsqrt(jnp.mean(shifted * shifted, axis=-1, keepdims=True) + EPSILON)
    return shifted * scale, scale


def norm_back(stream, gain, out_grad):
    xhat, scale = normalize(stream)
    u = out_grad * gain
    mean_u = jnp.mean(u, axis=-1, keepdims=True)
    mean_ux = jnp.mean(u * xhat, axis=-1, keepdims=True)
    return scale * (u - mean_u - xhat * mean_ux), jnp.sum(out_grad * xhat, axis=0, keepdims=True)


def both(own_ref, got_ref):
    return own_ref[...].astype(F32) + got_ref[...].astype(F32)


VMEM_SPEC = pl.BlockSpec(memory_space=pltpu.VMEM)
SMEM_SPEC = pl.BlockSpec(memory_space=pltpu.SMEM)
ANY_SPEC = pl.BlockSpec(memory_space=pl.ANY)


def call(body, outs, args, specs, scratch=(), flops=0, limit=40):
    outs = [jax.ShapeDtypeStruct(s, d) for s, d in outs]
    size = sum(o.size * o.dtype.itemsize for o in outs)
    size += sum(a.size * a.dtype.itemsize for a in args)
    return pl.pallas_call(
        body,
        grid=(1,),
        out_shape=outs,
        in_specs=specs,
        out_specs=[VMEM_SPEC] * len(outs),
        scratch_shapes=list(scratch),
        compiler_params=pltpu.CompilerParams(vmem_limit_bytes=limit << 20),
        cost_estimate=pl.CostEstimate(flops=flops, bytes_accessed=size, transcendentals=0),
    )(*args)


def layer_spec(shape, layer):
    return pl.BlockSpec(shape, lambda step: (layer,) + (0,) * (len(shape) - 1))


def place_kernel(slot_half, where_ref, routes_ref, place_ref):
    layers, _, rows = routes_ref.shape
    experts = place_ref.shape[1] // slot_half
    first = where_ref[0] * slot_half
    before_of = lax.broadcasted_iota(jnp.int32, (rows, rows), 0) < lax.broadcasted_iota(
        jnp.int32, (rows, rows), 1
    )
    earlier = jnp.where(before_of, 1.0, 0.0).astype(BF16)
    labels = lax.broadcasted_iota(jnp.int32, (experts, rows), 0)
    slots = lax.broadcasted_iota(jnp.int32, (slot_half, rows), 0)
    for layer in range(layers):
        named = (labels == routes_ref[layer, 0:1, :]) | (labels == routes_ref[layer, 1:2, :])
        count = mm(jnp.where(named, 1.0, 0.0).astype(BF16), earlier)
        slot = jnp.where(named, count.astype(jnp.int32) - first, -1)
        for e in range(experts):
            hit = slots == slot[e : e + 1, :]
            place_ref[layer, e * slot_half : (e + 1) * slot_half, :] = jnp.where(
                hit, 1.0, 0.0
            ).astype(BF16)


def pack_kernel(place_ref, rows_ref, out_ref):
    out_ref[...] = mm(place_ref[0], rows_ref[...]).astype(BF16)


def unpack_kernel(place_ref, got_ref, out_ref):
    out_ref[...] = mm_tn(place_ref[0], got_ref[...]).astype(BF16)


def pair_masks():
    lane = lax.broadcasted_iota(jnp.int32, (PAD, PAIR), 1)
    return lane < HEAD_DIM


def softmax_rows(q, k):
    scores = mm_nt(q, k) * HEAD_DIM ** (-0.5)
    column = lax.broadcasted_iota(jnp.int32, scores.shape, 1)
    scores = jnp.where(column < SEQ, scores, -1e30)
    top = jnp.max(scores, axis=-1, keepdims=True)
    weights = jnp.exp(scores - top)
    return weights / jnp.sum(weights, axis=-1, keepdims=True)


def attend_kernel(first, *refs):
    if first:
        tokens_ref, gain_ref, qkv_ref, wo_ref, h_ref, a_ref, proj_ref, mixed_ref, out_ref = refs
        h = tokens_ref[...].astype(F32)
    else:
        mid_ref, own_ref, got_ref, gain_ref, qkv_ref, wo_ref = refs[:6]
        h_ref, a_ref, proj_ref, mixed_ref, out_ref = refs[6:]
        h = mid_ref[...] + both(own_ref, got_ref)
    h_ref[...] = h
    a = (normalize(h)[0] * gain_ref[0, 0:1, :]).astype(BF16)
    a_ref[...] = a
    for c in range(3):
        proj_ref[c] = mm(a, qkv_ref[0, c]).astype(BF16)
    low = pair_masks()
    zero = jnp.zeros((PAD, PAIR), BF16)
    for image in range(a.shape[0] // PAD):
        rows = slice(image * PAD, (image + 1) * PAD)
        for pair in range(proj_ref.shape[2] // PAIR):
            lanes = slice(pair * PAIR, (pair + 1) * PAIR)
            q, k, v = (proj_ref[c, rows, lanes] for c in range(3))
            p0 = softmax_rows(jnp.where(low, q, zero), k).astype(BF16)
            p1 = softmax_rows(jnp.where(low, zero, q), k).astype(BF16)
            mixed_ref[rows, lanes] = jnp.where(low, mm(p0, v), mm(p1, v)).astype(BF16)
    out_ref[...] = mm(mixed_ref[...], wo_ref[0]).astype(BF16)


def route_kernel(h_ref, own_ref, got_ref, gain_ref, place_ref, mid_ref, send_ref):
    mid = h_ref[...] + both(own_ref, got_ref)
    mid_ref[...] = mid
    z = (normalize(mid)[0] * gain_ref[0, 1:2, :]).astype(BF16)
    send_ref[...] = mm(place_ref[0], z).astype(BF16)


def weight_copies(layer, core, win_own, win_a, win_b, wout_own, wout_a, wout_b, win, wout, sems):
    part = win.shape[2]
    copies = []
    for c in range(2):
        copies.append((win_own.at[layer, 0, :, pl.ds(c * part, part)], win.at[c]))
        copies.append((wout_own.at[layer, 0, pl.ds(c * part, part), :], wout.at[c]))
    copies.append((win_a, win.at[2 + core]))
    copies.append((wout_a, wout.at[2 + core]))
    copies.append((win_b, win.at[3 - core]))
    copies.append((wout_b, wout.at[3 - core]))
    return [pltpu.make_async_copy(s, d, sems.at[i]) for i, (s, d) in enumerate(copies)]


def expert_kernel(
    layer, where_ref, x_ref, router_ref, win_own, win_a, win_b, wout_own, wout_a, wout_b,
    out_ref, act_ref, slope_ref, gate_ref, win, wout, total, sems,
):
    copies = weight_copies(
        layer, where_ref[2], win_own, win_a, win_b, wout_own, wout_a, wout_b, win, wout, sems
    )
    for copy in copies:
        copy.start()
    x = x_ref[...]
    part = win.shape[2]
    logits = mm_nt(x, router_ref[...])
    gate = jnp.exp(logits - jnp.max(logits, axis=-1, keepdims=True))
    gate = gate / jnp.sum(gate, axis=-1, keepdims=True)
    gate_ref[...] = gate
    mine = lax.broadcasted_iota(jnp.int32, gate.shape, 1) == where_ref[1]
    share = jnp.sum(jnp.where(mine, gate, 0.0), axis=-1, keepdims=True)
    for c in range(4):
        if c == 2:
            for copy in copies[4:]:
                copy.wait()
        if c < 2:
            copies[2 * c].wait()
        pre = mm(x, win[c])
        square = pre * pre
        bent = jnp.tanh(GELU_A * pre * (1.0 + GELU_B * square))
        half = 0.5 * (1.0 + bent)
        act = (pre * half).astype(BF16)
        slope = half + (0.5 * GELU_A) * pre * (1.0 - bent * bent) * (1.0 + 3 * GELU_B * square)
        act_ref[:, c * part : (c + 1) * part] = act
        slope_ref[:, c * part : (c + 1) * part] = slope.astype(BF16)
        if c < 2:
            copies[2 * c + 1].wait()
        term = mm(act, wout[c])
        if c == 0:
            total[...] = term
        elif c < 3:
            total[...] += term
        else:
            out_ref[...] = (share * (total[...] + term)).astype(BF16)


def expert_back_kernel(
    layer, where_ref, g_ref, x_ref, act_ref, slope_ref, gate_ref, router_ref,
    win_own, win_a, win_b, wout_own, wout_a, wout_b,
    out_ref, pre_grad_ref, scaled_ref, router_grad_ref, win, wout, total, sems,
):
    copies = weight_copies(
        layer, where_ref[2], win_own, win_a, win_b, wout_own, wout_a, wout_b, win, wout, sems
    )
    for copy in copies:
        copy.start()
    g = g_ref[...]
    part = win.shape[2]
    gate = gate_ref[...]
    mine = lax.broadcasted_iota(jnp.int32, gate.shape, 1) == where_ref[1]
    share = jnp.sum(jnp.where(mine, gate, 0.0), axis=-1, keepdims=True)
    scaled_ref[...] = (share * g.astype(F32)).astype(BF16)
    dot = jnp.zeros(share.shape, F32)
    for c in range(4):
        cols = slice(c * part, (c + 1) * part)
        if c == 2:
            for copy in copies[4:]:
                copy.wait()
        if c < 2:
            copies[2 * c + 1].wait()
        u = mm_nt(g, wout[c])
        dot = dot + jnp.sum(u * act_ref[:, cols].astype(F32), axis=-1, keepdims=True)
        pre_grad = (share * u * slope_ref[:, cols].astype(F32)).astype(BF16)
        pre_grad_ref[:, cols] = pre_grad
        if c < 2:
            copies[2 * c].wait()
        term = mm_nt(pre_grad, win[c])
        if c == 0:
            total[...] = term
        else:
            total[...] += term
    logit_grad = (dot * share * (jnp.where(mine, 1.0, 0.0) - gate)).astype(BF16)
    router_grad_ref[...] = mm_tn(logit_grad, x_ref[...])
    out_ref[...] = (total[...] + mm(logit_grad, router_ref[...])).astype(BF16)


def attend_back_kernel(
    own_ref, got_ref, mid_ref, gain_ref, g_ref, a_ref, proj_ref, mixed_ref, qkv_ref, wo_ref,
    g_out_ref, gain_grad_ref, weight_grad_ref, out_ref, back_ref, mixed_grad_ref,
):
    h_grad, gain_grad_ref[...] = norm_back(
        mid_ref[...], gain_ref[0, 1:2, :], both(own_ref, got_ref)
    )
    g = g_ref[...].astype(F32) + h_grad
    g_out_ref[...] = g
    out_grad = g.astype(BF16)
    width = proj_ref.shape[2]
    depth = a_ref.shape[1]
    mixed_grad_ref[...] = mm_nt(out_grad, wo_ref[0]).astype(BF16)
    low = pair_masks()
    zero = jnp.zeros((PAD, PAIR), BF16)
    for image in range(g.shape[0] // PAD):
        rows = slice(image * PAD, (image + 1) * PAD)
        for pair in range(width // PAIR):
            lanes = slice(pair * PAIR, (pair + 1) * PAIR)
            q, k, v = (proj_ref[c, rows, lanes] for c in range(3))
            dm = mixed_grad_ref[rows, lanes]
            parts = []
            for side in range(2):
                def pick(t, side=side):
                    return jnp.where(low, t, zero) if side == 0 else jnp.where(low, zero, t)

                probs = softmax_rows(pick(q), k)
                prob_grad = mm_nt(pick(dm), v)
                row = jnp.sum(prob_grad * probs, axis=-1, keepdims=True)
                score_grad = (probs * (prob_grad - row)).astype(BF16)
                parts.append(
                    (
                        mm(score_grad, k) * HEAD_DIM ** (-0.5),
                        mm_tn(score_grad, q) * HEAD_DIM ** (-0.5),
                        mm_tn(probs.astype(BF16), dm),
                    )
                )
            for c in range(3):
                back_ref[c, rows, lanes] = jnp.where(low, parts[0][c], parts[1][c]).astype(BF16)
    total = mm_nt(back_ref[0], qkv_ref[0, 0])
    total += mm_nt(back_ref[1], qkv_ref[0, 1])
    total += mm_nt(back_ref[2], qkv_ref[0, 2])
    out_ref[...] = total.astype(BF16)
    for c in range(3):
        weight_grad_ref[c * depth : (c + 1) * depth, :] = mm_tn(a_ref[...], back_ref[c]).astype(BF16)
    proj_grad = mm_tn(mixed_ref[...], out_grad)
    for c in range(depth // width):
        start = 3 * depth + c * width
        weight_grad_ref[start : start + width, :] = proj_grad[
            :, c * width : (c + 1) * width
        ].astype(BF16)


def stream_back_kernel(pack, *refs):
    if pack:
        own_ref, got_ref, h_ref, gain_ref, g_ref, place_ref, g_out_ref, gain_grad_ref, send_ref = refs
    else:
        own_ref, got_ref, h_ref, gain_ref, g_ref, g_out_ref, gain_grad_ref = refs
    h_grad, gain_grad_ref[...] = norm_back(h_ref[...], gain_ref[0, 0:1, :], both(own_ref, got_ref))
    g = g_ref[...] + h_grad
    g_out_ref[...] = g
    if pack:
        send_ref[...] = mm(place_ref[0], g.astype(BF16)).astype(BF16)


def swap(value, axis):
    return lax.ppermute(value, axis, [(0, 1), (1, 0)])


def on_device(tokens, gains, attn_qkv, attn_out, router, expert_in, expert_out, routes, cotangent):
    row_count, width = tokens.shape
    layers = attn_qkv.shape[0]
    local = attn_qkv.shape[3]
    images = row_count // SEQ
    rows = images * PAD
    experts = router.shape[2]
    hidden = expert_in.shape[3]
    part = hidden // 2
    capacity = 8 * (5 * row_count // (16 * experts) + 1)
    slot_half = capacity // 2
    slots = experts * slot_half
    side = lax.axis_index("tensor")
    core = lax.axis_index("replica")
    where = jnp.stack([side, lax.axis_index("expert"), core]).astype(jnp.int32)

    def spread(array):
        array = array.reshape(images, SEQ, width)
        return jnp.pad(array, ((0, 0), (0, PAD - SEQ), (0, 0))).reshape(rows, width)

    def gathered(array):
        return array.reshape(images, PAD, width)[:, :SEQ].reshape(row_count, width)

    def exchange(block):
        block = block.reshape(experts, slot_half, width)
        return lax.all_to_all(block, "expert", 0, 0, tiled=True).reshape(slots, width)

    whole = []
    for layer in range(layers):
        piece_in = lax.dynamic_slice(
            expert_in, (layer, 0, 0, core * part), (1, 1, width, part)
        ).reshape(width, part)
        piece_out = lax.dynamic_slice(
            expert_out, (layer, 0, core * part, 0), (1, 1, part, width)
        ).reshape(part, width)
        in_a, out_a = swap(piece_in, "tensor"), swap(piece_out, "tensor")
        whole.append((expert_in, in_a, swap(in_a, "replica"), expert_out, out_a, swap(out_a, "replica")))

    routes_t = jnp.swapaxes(routes, 1, 2).reshape(layers, 2, images, SEQ)
    routes_t = jnp.pad(
        routes_t, ((0, 0), (0, 0), (0, 0), (0, PAD - SEQ)), constant_values=-1
    ).reshape(layers, 2, rows)
    [place] = call(
        functools.partial(place_kernel, slot_half),
        [((layers, slots, rows), BF16)],
        (where, routes_t),
        [SMEM_SPEC, VMEM_SPEC],
        flops=2 * layers * rows * rows * experts,
    )
    router_t = jnp.swapaxes(router, 1, 2)

    def place_spec(layer):
        return layer_spec((1, slots, rows), layer)

    def gain_spec(layer):
        return layer_spec((1, 2, width), layer)

    pack_flops = 2 * slots * rows * width
    weight_scratch = [
        pltpu.VMEM((4, width, part), BF16),
        pltpu.VMEM((4, part, width), BF16),
        pltpu.VMEM((slots, width), F32),
        pltpu.SemaphoreType.DMA((8,)),
    ]
    expert_flops = 8 * slots * width * hidden

    upstream = spread(cotangent)
    last = layers - 1
    [send] = call(
        pack_kernel,
        [((slots, width), BF16)],
        (place, upstream),
        [place_spec(last), VMEM_SPEC],
        flops=pack_flops,
    )
    received_grad = exchange(send)

    stream_args = (spread(tokens),)
    saved = []
    for layer in range(layers):
        h, a, proj, mixed, term = call(
            functools.partial(attend_kernel, layer == 0),
            [
                ((rows, width), F32),
                ((rows, width), BF16),
                ((3, rows, local), BF16),
                ((rows, local), BF16),
                ((rows, width), BF16),
            ],
            (*stream_args, gains, attn_qkv, attn_out),
            [
                *([VMEM_SPEC] * len(stream_args)),
                gain_spec(layer),
                layer_spec((1, 3, width, local), layer),
                layer_spec((1, local, width), layer),
            ],
            flops=8 * rows * width * local + 4 * rows * PAD * local,
        )
        mid, send = call(
            route_kernel,
            [((rows, width), F32), ((slots, width), BF16)],
            (h, term, swap(term, "tensor"), gains, place),
            [VMEM_SPEC] * 3 + [gain_spec(layer), place_spec(layer)],
            flops=pack_flops,
        )
        received = exchange(send)
        reply, act, slope, gate = call(
            functools.partial(expert_kernel, layer),
            [
                ((slots, width), BF16),
                ((slots, 2 * hidden), BF16),
                ((slots, 2 * hidden), BF16),
                ((slots, experts), F32),
            ],
            (where, received, router_t[layer], *whole[layer]),
            [SMEM_SPEC, VMEM_SPEC, VMEM_SPEC] + [ANY_SPEC] * 6,
            weight_scratch,
            flops=expert_flops,
            limit=56,
        )
        returned = exchange(reply)
        [term] = call(
            unpack_kernel,
            [((rows, width), BF16)],
            (place, returned),
            [place_spec(layer), VMEM_SPEC],
            flops=pack_flops,
        )
        stream_args = (mid, term, swap(term, "tensor"))
        saved.append((h, a, proj, mixed, mid, received, act, slope, gate))
    mid, own, got = stream_args
    mixed_out = gathered((mid + (own.astype(F32) + got.astype(F32))).astype(BF16))

    grads = [None] * layers
    for layer in reversed(range(layers)):
        h, a, proj, mixed, mid, received, act, slope, gate = saved[layer]
        reply, pre_grad, scaled, router_grad = call(
            functools.partial(expert_back_kernel, layer),
            [
                ((slots, width), BF16),
                ((slots, 2 * hidden), BF16),
                ((slots, width), BF16),
                ((experts, width), F32),
            ],
            (where, received_grad, received, act, slope, gate, router_t[layer], *whole[layer]),
            [SMEM_SPEC] + [VMEM_SPEC] * 6 + [ANY_SPEC] * 6,
            weight_scratch,
            flops=expert_flops,
            limit=56,
        )
        returned = exchange(reply)

        half = width // 2

        def columns(array, which):
            return lax.dynamic_slice_in_dim(array, which * half, half, axis=1)

        def dot_t(left, right):
            return lax.dot_general(left, right, TN, preferred_element_type=F32)

        x_mine, x_other = columns(received, core), columns(received, 1 - core)
        s_mine, s_other = columns(scaled, core), columns(scaled, 1 - core)
        in_got = swap(dot_t(x_other, pre_grad).astype(BF16), "replica").astype(F32)
        out_got = swap(dot_t(act, s_other).astype(BF16), "replica").astype(F32)
        in_far = (dot_t(x_mine, pre_grad[:, hidden:]) + in_got[:, hidden:]).astype(BF16)
        out_far = (dot_t(act[:, hidden:], s_mine) + out_got[hidden:]).astype(BF16)
        in_far, out_far = swap(in_far, "tensor"), swap(out_far, "tensor")
        grad_in = dot_t(x_mine, pre_grad[:, :hidden]) + in_got[:, :hidden] + in_far.astype(F32)
        grad_out = dot_t(act[:, :hidden], s_mine) + out_got[:hidden] + out_far.astype(F32)

        [term] = call(
            unpack_kernel,
            [((rows, width), BF16)],
            (place, returned),
            [place_spec(layer), VMEM_SPEC],
            flops=pack_flops,
        )
        upstream, gain_two, weight_grad, term = call(
            attend_back_kernel,
            [
                ((rows, width), F32),
                ((1, width), F32),
                ((4 * width, local), BF16),
                ((rows, width), BF16),
            ],
            (term, swap(term, "tensor"), mid, gains, upstream, a, proj, mixed, attn_qkv, attn_out),
            [VMEM_SPEC] * 3
            + [gain_spec(layer)]
            + [VMEM_SPEC] * 4
            + [layer_spec((1, 3, width, local), layer), layer_spec((1, local, width), layer)],
            [pltpu.VMEM((3, rows, local), BF16), pltpu.VMEM((rows, local), BF16)],
            flops=16 * rows * width * local + 10 * rows * PAD * local,
        )
        halves = weight_grad.reshape(2, 2 * width, local)
        got = swap(lax.dynamic_index_in_dim(halves, 1 - core, keepdims=False), "replica")
        mine = lax.dynamic_index_in_dim(halves, core, keepdims=False)
        mine = (mine.astype(F32) + got.astype(F32)).astype(BF16)
        mine = mine.reshape(experts, 2 * width // experts, local)
        mine = lax.all_to_all(mine, "expert", 0, 0, tiled=True)
        mine = jnp.sum(mine.astype(F32), axis=0, keepdims=True).astype(BF16)
        mine = jnp.broadcast_to(mine, (experts, 2 * width // experts, local))
        mine = lax.all_to_all(mine, "expert", 0, 0, tiled=True).reshape(2 * width, local)
        got = swap(mine, "replica")
        lower = jnp.where(core == 0, mine, got).astype(F32)
        upper = jnp.where(core == 0, got, mine).astype(F32)
        grad_qkv = jnp.concatenate([lower, upper[:width]]).reshape(3, width, local)
        grad_proj = jnp.concatenate([upper[width : width + local], upper[width + local :]], axis=1)

        got = swap(term, "tensor")
        if layer > 0:
            upstream, gain_one, send = call(
                functools.partial(stream_back_kernel, True),
                [((rows, width), F32), ((1, width), F32), ((slots, width), BF16)],
                (term, got, h, gains, upstream, place),
                [VMEM_SPEC] * 3 + [gain_spec(layer), VMEM_SPEC, place_spec(layer - 1)],
                flops=pack_flops,
            )
            received_grad = exchange(send)
        else:
            upstream, gain_one = call(
                functools.partial(stream_back_kernel, False),
                [((rows, width), F32), ((1, width), F32)],
                (term, got, h, gains, upstream),
                [VMEM_SPEC] * 3 + [gain_spec(layer), VMEM_SPEC],
            )
        gain_pair = jnp.where(side == 0, jnp.concatenate([gain_one, gain_two]), 0.0)
        small = jnp.concatenate([router_grad, gain_pair])
        grads[layer] = (small, grad_qkv, grad_proj, grad_in, grad_out)

    small, grad_qkv, grad_proj, grad_in, grad_out = (
        jnp.stack([item[position] for item in grads]) for position in range(5)
    )
    small = lax.psum(small, ("tensor", "expert", "replica"))
    return (
        mixed_out,
        gathered(upstream),
        small[:, experts:],
        grad_qkv,
        grad_proj,
        jnp.swapaxes(small[:, :experts], 1, 2),
        grad_in[:, None],
        grad_out[:, None],
    )


def solution(mesh):
    return jax.shard_map(
        on_device,
        mesh=mesh,
        in_specs=(
            P(("expert", "replica"), None),
            P(),
            P(None, None, None, "tensor"),
            P(None, "tensor", None),
            P(),
            P(None, "expert", None, "tensor"),
            P(None, "expert", "tensor", None),
            P(None, ("expert", "replica"), None),
            P(("expert", "replica"), None),
        ),
        out_specs=(
            P(("expert", "replica"), None),
            P(("expert", "replica"), None),
            P(),
            P(None, None, None, "tensor"),
            P(None, "tensor", None),
            P(),
            P(None, "expert", "replica", "tensor"),
            P(None, "expert", "tensor", "replica"),
        ),
        check_vma=False,
    )
```

```python
import functools

import jax
import jax.numpy as jnp
from jax import lax
from jax.experimental import pallas as pl
from jax.experimental.pallas import tpu as pltpu
from jax.sharding import PartitionSpec as P

HEAD_DIM = 64
SEQ = 197
PAD = 208
PAIR = 2 * HEAD_DIM
EPSILON = 1e-06
GELU_A = 0.7978845608028654
GELU_B = 0.044715
F32 = jnp.float32
BF16 = jnp.bfloat16
NT = (((1,), (1,)), ((), ()))
TN = (((0,), (0,)), ((), ()))


def mm(a, b):
    return jnp.dot(a, b, preferred_element_type=F32)


def mm_nt(a, b):
    return lax.dot_general(a, b, NT, preferred_element_type=F32)


def mm_tn(a, b):
    return lax.dot_general(a, b, TN, preferred_element_type=F32)


def normalize(stream):
    shifted = stream - jnp.mean(stream, axis=-1, keepdims=True)
    scale = lax.rsqrt(jnp.mean(shifted * shifted, axis=-1, keepdims=True) + EPSILON)
    return shifted * scale, scale


def norm_back(stream, gain, out_grad):
    xhat, scale = normalize(stream)
    u = out_grad * gain
    mean_u = jnp.mean(u, axis=-1, keepdims=True)
    mean_ux = jnp.mean(u * xhat, axis=-1, keepdims=True)
    return scale * (u - mean_u - xhat * mean_ux), jnp.sum(out_grad * xhat, axis=0, keepdims=True)


def both(own_ref, got_ref):
    return own_ref[...].astype(F32) + got_ref[...].astype(F32)


VMEM_SPEC = pl.BlockSpec(memory_space=pltpu.VMEM)
SMEM_SPEC = pl.BlockSpec(memory_space=pltpu.SMEM)
ANY_SPEC = pl.BlockSpec(memory_space=pl.ANY)


def call(body, outs, args, specs, scratch=(), flops=0, limit=40, deps=(), grid=(1,), alias=None):
    out_specs = [o[2] if len(o) > 2 else VMEM_SPEC for o in outs]
    outs = [jax.ShapeDtypeStruct(o[0], o[1]) for o in outs]
    size = sum(o.size * o.dtype.itemsize for o in outs)
    size += sum(a.size * a.dtype.itemsize for a in args)
    taken, last = len(args), len(args) + len(deps)

    def kernel(*refs):
        body(*refs[:taken], *refs[last:])

    return pl.pallas_call(
        kernel,
        grid=grid,
        out_shape=outs,
        in_specs=[*specs, *([ANY_SPEC] * len(deps))],
        out_specs=out_specs,
        scratch_shapes=list(scratch),
        input_output_aliases=alias or {},
        compiler_params=pltpu.CompilerParams(vmem_limit_bytes=limit << 20),
        cost_estimate=pl.CostEstimate(flops=flops, bytes_accessed=size, transcendentals=0),
    )(*args, *deps)


def layer_spec(shape, layer):
    return pl.BlockSpec(shape, lambda step: (layer,) + (0,) * (len(shape) - 1))


def place_kernel(slot_half, where_ref, routes_ref, rows_ref, place_ref, send_ref):
    layers, _, rows = routes_ref.shape
    experts = place_ref.shape[1] // slot_half
    first = where_ref[0] * slot_half
    before_of = lax.broadcasted_iota(jnp.int32, (rows, rows), 0) < lax.broadcasted_iota(
        jnp.int32, (rows, rows), 1
    )
    earlier = jnp.where(before_of, 1.0, 0.0).astype(BF16)
    labels = lax.broadcasted_iota(jnp.int32, (experts, rows), 0)
    slots = lax.broadcasted_iota(jnp.int32, (slot_half, rows), 0)
    for layer in range(layers):
        named = (labels == routes_ref[layer, 0:1, :]) | (labels == routes_ref[layer, 1:2, :])
        count = mm(jnp.where(named, 1.0, 0.0).astype(BF16), earlier)
        slot = jnp.where(named, count.astype(jnp.int32) - first, -1)
        for e in range(experts):
            hit = slots == slot[e : e + 1, :]
            place_ref[layer, e * slot_half : (e + 1) * slot_half, :] = jnp.where(
                hit, 1.0, 0.0
            ).astype(BF16)
    send_ref[...] = mm(place_ref[layers - 1], rows_ref[...]).astype(BF16)


def piece_of(matrix_in, matrix_out, layer, core):
    if matrix_in is not None:
        part = matrix_in.shape[3] // 2
        return matrix_in.at[layer, 0, :, pl.ds(pl.multiple_of(core * part, part), part)]
    part = matrix_out.shape[2] // 2
    return matrix_out.at[layer, 0, pl.ds(pl.multiple_of(core * part, part), part), :]


def fetch_kernel(layer, where_ref, source_ref, piece_ref, sem):
    copy = pltpu.make_async_copy(
        piece_of(source_ref, None, layer, where_ref[2]), piece_ref, sem.at[0]
    )
    copy.start()
    copy.wait()


def unpack_kernel(place_ref, got_ref, out_ref):
    out_ref[...] = mm_tn(place_ref[0], got_ref[...]).astype(BF16)


def unpack_pass_kernel(place_ref, got_ref, reply_ref, out_ref, passed_ref, sem):
    copy = pltpu.make_async_copy(reply_ref, passed_ref, sem.at[0])
    copy.start()
    out_ref[...] = mm_tn(place_ref[0], got_ref[...]).astype(BF16)
    copy.wait()


def pair_masks():
    lane = lax.broadcasted_iota(jnp.int32, (PAD, PAIR), 1)
    return lane < HEAD_DIM


def softmax_rows(q, k):
    scores = mm_nt(q, k) * HEAD_DIM ** (-0.5)
    column = lax.broadcasted_iota(jnp.int32, scores.shape, 1)
    scores = jnp.where(column < SEQ, scores, -1e30)
    top = jnp.max(scores, axis=-1, keepdims=True)
    weights = jnp.exp(scores - top)
    return weights / jnp.sum(weights, axis=-1, keepdims=True)


def attend_kernel(first, *refs):
    if first:
        tokens_ref, gain_ref, qkv_ref, wo_ref, h_ref, a_ref, proj_ref, mixed_ref, out_ref = refs
        h = tokens_ref[...].astype(F32)
    else:
        mid_ref, own_ref, got_ref, gain_ref, qkv_ref, wo_ref = refs[:6]
        h_ref, a_ref, proj_ref, mixed_ref, out_ref = refs[6:]
        h = mid_ref[...] + both(own_ref, got_ref)
    h_ref[...] = h
    a = (normalize(h)[0] * gain_ref[0, 0:1, :]).astype(BF16)
    a_ref[...] = a
    for c in range(3):
        proj_ref[c] = mm(a, qkv_ref[0, c]).astype(BF16)
    low = pair_masks()
    zero = jnp.zeros((PAD, PAIR), BF16)
    for image in range(a.shape[0] // PAD):
        rows = slice(image * PAD, (image + 1) * PAD)
        for pair in range(proj_ref.shape[2] // PAIR):
            lanes = slice(pair * PAIR, (pair + 1) * PAIR)
            q, k, v = (proj_ref[c, rows, lanes] for c in range(3))
            p0 = softmax_rows(jnp.where(low, q, zero), k).astype(BF16)
            p1 = softmax_rows(jnp.where(low, zero, q), k).astype(BF16)
            mixed_ref[rows, lanes] = jnp.where(low, mm(p0, v), mm(p1, v)).astype(BF16)
    out_ref[...] = mm(mixed_ref[...], wo_ref[0]).astype(BF16)


def route_kernel(
    layer, where_ref, h_ref, own_ref, got_ref, gain_ref, place_ref, source_ref, mid_ref, send_ref, piece_ref, sem
):
    copy = pltpu.make_async_copy(
        piece_of(None, source_ref, layer, where_ref[2]), piece_ref, sem.at[0]
    )
    copy.start()
    mid = h_ref[...] + both(own_ref, got_ref)
    mid_ref[...] = mid
    z = (normalize(mid)[0] * gain_ref[0, 1:2, :]).astype(BF16)
    send_ref[...] = mm(place_ref[0], z).astype(BF16)
    copy.wait()


def load_weights(layer, core, sources, win, wout, sems, in_first):
    win_own, win_a, win_b, wout_own, wout_a, wout_b = sources
    part = win.shape[2]
    groups = []
    for c in range(2):
        groups.append(
            [
                (win_own.at[layer, 0, :, pl.ds(c * part, part)], win.at[c], 2 * c),
                (wout_own.at[layer, 0, pl.ds(c * part, part), :], wout.at[c], 2 * c + 1),
            ]
        )
    groups.append(
        [
            (win_a, win.at[2 + core], 4),
            (wout_a, wout.at[2 + core], 5),
            (win_b, win.at[3 - core], 6),
            (wout_b, wout.at[3 - core], 7),
        ]
    )
    groups = [[pltpu.make_async_copy(s, d, sems.at[i]) for s, d, i in group] for group in groups]

    @pl.when(pl.program_id(0) == 0)
    def _():
        for group in groups:
            for copy in group:
                copy.start()

    for step, group in enumerate(groups):

        @pl.when(pl.program_id(0) == step)
        def _(group=group):
            for copy in group:
                copy.wait()


def gate_of(x, router, expert):
    logits = mm_nt(x, router)
    gate = jnp.exp(logits - jnp.max(logits, axis=-1, keepdims=True))
    gate = gate / jnp.sum(gate, axis=-1, keepdims=True)
    mine = lax.broadcasted_iota(jnp.int32, gate.shape, 1) == expert
    return gate, mine, jnp.sum(jnp.where(mine, gate, 0.0), axis=-1, keepdims=True)


def bend(pre):
    square = pre * pre
    bent = jnp.tanh(pre * (GELU_A + (GELU_A * GELU_B) * square))
    half = 0.5 + 0.5 * bent
    slope = half + pre * (1.0 - bent * bent) * (0.5 * GELU_A + (1.5 * GELU_A * GELU_B) * square)
    return pre * half, slope


def add_step(total, term):
    @pl.when(pl.program_id(0) == 0)
    def _():
        total[...] = term

    @pl.when(pl.program_id(0) > 0)
    def _():
        total[...] += term


def expert_kernel(
    layer, where_ref, x_ref, router_ref, win_own, win_a, win_b, wout_own, wout_a, wout_b,
    out_ref, act_ref, slope_ref, win, wout, total, sems,
):
    step = pl.program_id(0)
    sources = (win_own, win_a, win_b, wout_own, wout_a, wout_b)
    load_weights(layer, where_ref[2], sources, win, wout, sems, True)
    act, slope = bend(mm(x_ref[...], win[step]))
    act = act.astype(BF16)
    act_ref[...] = act
    slope_ref[...] = slope.astype(BF16)
    add_step(total, mm(act, wout[step]))

    @pl.when(step == pl.num_programs(0) - 1)
    def _():
        _, _, share = gate_of(x_ref[...], router_ref[...], where_ref[1])
        out_ref[...] = (share * total[...]).astype(BF16)


def finish_back(x_ref, router_ref, gate, mine, share, dot, total, out_ref, router_grad_ref):
    logit_grad = (dot * share * (jnp.where(mine, 1.0, 0.0) - gate)).astype(BF16)
    router_grad_ref[...] = mm_tn(logit_grad, x_ref[...])
    out_ref[...] = (total + mm(logit_grad, router_ref[...])).astype(BF16)


def expert_back_kernel(
    layer, where_ref, g_ref, x_ref, act_ref, slope_ref, router_ref,
    win_own, win_a, win_b, wout_own, wout_a, wout_b,
    out_ref, pre_grad_ref, scaled_ref, router_grad_ref, win, wout, total, dot_ref, sems,
):
    step = pl.program_id(0)
    sources = (win_own, win_a, win_b, wout_own, wout_a, wout_b)
    load_weights(layer, where_ref[2], sources, win, wout, sems, False)
    g = g_ref[...]
    gate, mine, share = gate_of(x_ref[...], router_ref[...], where_ref[1])
    u = mm_nt(g, wout[step])
    pre_grad = (share * u * slope_ref[...].astype(F32)).astype(BF16)
    pre_grad_ref[...] = pre_grad
    add_step(total, mm_nt(pre_grad, win[step]))
    add_step(dot_ref, jnp.sum(u * act_ref[...].astype(F32), axis=-1, keepdims=True))

    @pl.when(step == pl.num_programs(0) - 1)
    def _():
        scaled_ref[...] = (share * g.astype(F32)).astype(BF16)
        finish_back(
            x_ref, router_ref, gate, mine, share, dot_ref[...], total[...], out_ref, router_grad_ref
        )


def expert_both_kernel(
    layer, where_ref, g_ref, x_ref, router_ref,
    win_own, win_a, win_b, wout_own, wout_a, wout_b,
    out_ref, back_ref, act_ref, pre_grad_ref, scaled_ref, router_grad_ref,
    win, wout, total, back_total, dot_ref, sems,
):
    step = pl.program_id(0)
    sources = (win_own, win_a, win_b, wout_own, wout_a, wout_b)
    load_weights(layer, where_ref[2], sources, win, wout, sems, True)
    g = g_ref[...]
    gate, mine, share = gate_of(x_ref[...], router_ref[...], where_ref[1])
    act, slope = bend(mm(x_ref[...], win[step]))
    u = mm_nt(g, wout[step])
    act = act.astype(BF16)
    act_ref[...] = act
    pre_grad = (share * u * slope).astype(BF16)
    pre_grad_ref[...] = pre_grad
    add_step(total, mm(act, wout[step]))
    add_step(back_total, mm_nt(pre_grad, win[step]))
    add_step(dot_ref, jnp.sum(u * act.astype(F32), axis=-1, keepdims=True))

    @pl.when(step == pl.num_programs(0) - 1)
    def _():
        out_ref[...] = (share * total[...]).astype(BF16)
        scaled_ref[...] = (share * g.astype(F32)).astype(BF16)
        finish_back(
            x_ref, router_ref, gate, mine, share, dot_ref[...], back_total[...], back_ref, router_grad_ref
        )


def half_of(ref, which):
    half = ref.shape[1] // 2
    return ref[:, pl.ds(pl.multiple_of(which * half, half), half)]


def grad_other_kernel(where_ref, x_ref, scaled_ref, pre_grad_ref, act_ref, in_ref, out_ref):
    other = 1 - where_ref[2]
    in_ref[...] = mm_tn(half_of(x_ref, other), pre_grad_ref[...]).astype(BF16)
    out_ref[...] = mm_tn(act_ref[...], half_of(scaled_ref, other)).astype(BF16)


def grad_far_kernel(
    where_ref, x_ref, scaled_ref, pre_grad_ref, act_ref, in_got_ref, out_got_ref, in_ref, out_ref
):
    core = where_ref[2]
    term = mm_tn(half_of(x_ref, core), pre_grad_ref[...])
    in_ref[...] = (term + in_got_ref[...].astype(F32)).astype(BF16)
    term = mm_tn(act_ref[...], half_of(scaled_ref, core))
    out_ref[...] = (term + out_got_ref[...].astype(F32)).astype(BF16)


def grad_own_kernel(
    where_ref, x_ref, scaled_ref, pre_grad_ref, act_ref, in_got_ref, out_got_ref, in_far_ref, out_far_ref, *refs
):
    core = where_ref[2]
    in_ref, out_ref = refs[-2:]
    term = mm_tn(half_of(x_ref, core), pre_grad_ref[...])
    in_ref[0] = term + in_got_ref[...].astype(F32) + in_far_ref[...].astype(F32)
    term = mm_tn(act_ref[...], half_of(scaled_ref, core))
    out_ref[0] = term + out_got_ref[...].astype(F32) + out_far_ref[...].astype(F32)


def attend_back_kernel(
    where_ref, own_ref, got_ref, mid_ref, gain_ref, g_ref, a_ref, proj_ref, mixed_ref, qkv_ref, wo_ref,
    g_out_ref, gain_grad_ref, out_ref, *refs,
):
    back_ref, mixed_grad_ref = refs[-2:]
    h_grad, gain_grad_ref[...] = norm_back(
        mid_ref[...], gain_ref[0, 1:2, :], both(own_ref, got_ref)
    )
    g = g_ref[...].astype(F32) + h_grad
    g_out_ref[...] = g
    out_grad = g.astype(BF16)
    width = proj_ref.shape[2]
    depth = a_ref.shape[1]
    mixed_grad_ref[...] = mm_nt(out_grad, wo_ref[0]).astype(BF16)
    low = pair_masks()
    zero = jnp.zeros((PAD, PAIR), BF16)
    for image in range(g.shape[0] // PAD):
        rows = slice(image * PAD, (image + 1) * PAD)
        for pair in range(width // PAIR):
            lanes = slice(pair * PAIR, (pair + 1) * PAIR)
            q, k, v = (proj_ref[c, rows, lanes] for c in range(3))
            dm = mixed_grad_ref[rows, lanes]
            parts = []
            for side in range(2):
                def pick(t, side=side):
                    return jnp.where(low, t, zero) if side == 0 else jnp.where(low, zero, t)

                probs = softmax_rows(pick(q), k)
                prob_grad = mm_nt(pick(dm), v)
                row = jnp.sum(prob_grad * probs, axis=-1, keepdims=True)
                score_grad = (probs * (prob_grad - row)).astype(BF16)
                parts.append(
                    (
                        mm(score_grad, k) * HEAD_DIM ** (-0.5),
                        mm_tn(score_grad, q) * HEAD_DIM ** (-0.5),
                        mm_tn(probs.astype(BF16), dm),
                    )
                )
            for c in range(3):
                back_ref[c, rows, lanes] = jnp.where(low, parts[0][c], parts[1][c]).astype(BF16)
    total = mm_nt(back_ref[0], qkv_ref[0, 0])
    total += mm_nt(back_ref[1], qkv_ref[0, 1])
    total += mm_nt(back_ref[2], qkv_ref[0, 2])
    out_ref[...] = total.astype(BF16)
    core = where_ref[2]

    def put(block, start, value):
        @pl.when(core == block // 2)
        def _():
            refs[0][start : start + value.shape[0], :] = value.astype(BF16)

        @pl.when(core != block // 2)
        def _():
            refs[1][start : start + value.shape[0], :] = value.astype(BF16)

    for c in range(3):
        put(c, c % 2 * depth, mm_tn(a_ref[...], back_ref[c]))
    proj_grad = mm_tn(mixed_ref[...], out_grad)
    for c in range(depth // width):
        put(3, depth + c * width, proj_grad[:, c * width : (c + 1) * width])


def stream_back_kernel(pack, *refs):
    if pack:
        own_ref, got_ref, h_ref, gain_ref, g_ref, place_ref, g_out_ref, gain_grad_ref, send_ref = refs
    else:
        own_ref, got_ref, h_ref, gain_ref, g_ref, g_out_ref, gain_grad_ref = refs
    h_grad, gain_grad_ref[...] = norm_back(h_ref[...], gain_ref[0, 0:1, :], both(own_ref, got_ref))
    g = g_ref[...] + h_grad
    g_out_ref[...] = g
    if pack:
        send_ref[...] = mm(place_ref[0], g.astype(BF16)).astype(BF16)


def swap(value, axis):
    return lax.ppermute(value, axis, [(0, 1), (1, 0)])


def partner(value, axis, bit):
    count = lax.axis_size(axis)
    return lax.ppermute(value, axis, [(i, i ^ (1 << bit)) for i in range(count)])


def split_kernel(sides_ref, keep_a_ref, got_a_ref, keep_b_ref, got_b_ref, *outs):
    for i, (keep_ref, got_ref) in enumerate(((keep_a_ref, got_a_ref), (keep_b_ref, got_b_ref))):
        out_ref, send_ref = outs[2 * i], outs[2 * i + 1]
        half = out_ref.shape[0]
        side = sides_ref[i]
        mine, other = pl.ds(side * half, half), pl.ds((1 - side) * half, half)
        out_ref[...] = keep_ref[mine].astype(F32) + got_ref[mine].astype(F32)
        send_ref[...] = (keep_ref[other].astype(F32) + got_ref[other].astype(F32)).astype(BF16)


def last_sum_kernel(keep_a_ref, got_a_ref, keep_b_ref, got_b_ref, a_ref, b_ref):
    a_ref[...] = both(keep_a_ref, got_a_ref).astype(BF16)
    b_ref[...] = both(keep_b_ref, got_b_ref).astype(BF16)


def join_kernel(sides_ref, own_a_ref, got_a_ref, own_b_ref, got_b_ref, a_ref, b_ref):
    pairs = ((own_a_ref, got_a_ref, a_ref), (own_b_ref, got_b_ref, b_ref))
    for i, (own_ref, got_ref, out_ref) in enumerate(pairs):
        half = own_ref.shape[0]
        side = sides_ref[i]
        out_ref[pl.ds(side * half, half)] = own_ref[...]
        out_ref[pl.ds((1 - side) * half, half)] = got_ref[...]


class ExpertSum:
    def __init__(self, mine, got, experts):
        rows, width = mine.shape
        block = rows // (2 * experts)
        mine, got = (v.reshape(2, experts, block, width) for v in (mine, got))
        bits = list(range(experts.bit_length() - 1))
        self.orders = list(zip(bits, [*bits[1::-1], *bits[2:]]))
        me = lax.axis_index("expert")
        self.sides = [jnp.stack([(me >> a) & 1, (me >> b) & 1]).astype(jnp.int32) for a, b in self.orders]
        self.state = (mine[0], got[0], mine[1], got[1])
        self.count, self.block, self.width = experts, block, width
        self.step = 0

    def shape(self):
        return (self.count, self.block, self.width)

    def split(self, deps=()):
        self.count //= 2
        a, b = self.orders[self.step]
        keep_a, send_a, keep_b, send_b = call(
            split_kernel,
            [(self.shape(), F32), (self.shape(), BF16)] * 2,
            (self.sides[self.step], *self.state),
            [SMEM_SPEC] + [VMEM_SPEC] * 4,
            deps=deps,
        )
        self.step += 1
        self.state = (keep_a, partner(send_a, "expert", a), keep_b, partner(send_b, "expert", b))
        return send_a

    def finish(self, deps=()):
        while self.step < len(self.orders):
            self.split()
        self.state = call(
            last_sum_kernel, [(self.shape(), BF16)] * 2, self.state, [VMEM_SPEC] * 4, deps=deps
        )
        return self.state[0]

    def join(self, deps=()):
        self.step -= 1
        own_a, own_b = self.state
        a, b = self.orders[self.step]
        got_a, got_b = partner(own_a, "expert", a), partner(own_b, "expert", b)
        self.count *= 2
        self.state = call(
            join_kernel,
            [(self.shape(), BF16)] * 2,
            (self.sides[self.step], own_a, got_a, own_b, got_b),
            [SMEM_SPEC] + [VMEM_SPEC] * 4,
            deps=deps,
        )
        return self.state[0]

    def result(self):
        while self.step:
            self.join()
        return jnp.concatenate(self.state).reshape(-1, self.width)


def sum_all(value):
    for bit in range(lax.axis_size("expert").bit_length() - 1):
        value = value + partner(value, "expert", bit)
    value = value + swap(value, "replica")
    return value + swap(value, "tensor")


def on_device(tokens, gains, attn_qkv, attn_out, router, expert_in, expert_out, routes, cotangent):
    row_count, width = tokens.shape
    layers = attn_qkv.shape[0]
    local = attn_qkv.shape[3]
    images = row_count // SEQ
    rows = images * PAD
    experts = router.shape[2]
    hidden = expert_in.shape[3]
    part = hidden // 2
    half = width // 2
    capacity = 8 * (5 * row_count // (16 * experts) + 1)
    slot_half = capacity // 2
    slots = experts * slot_half
    side = lax.axis_index("tensor")
    core = lax.axis_index("replica")
    where = jnp.stack([side, lax.axis_index("expert"), core]).astype(jnp.int32)
    last = layers - 1

    def spread(array):
        array = array.reshape(images, SEQ, width)
        return jnp.pad(array, ((0, 0), (0, PAD - SEQ), (0, 0))).reshape(rows, width)

    def gathered(array):
        return array.reshape(images, PAD, width)[:, :SEQ].reshape(row_count, width)

    def exchange(block):
        block = block.reshape(experts, slot_half, width)
        return lax.all_to_all(block, "expert", 0, 0, tiled=True).reshape(slots, width)

    def fetch(layer, deps=()):
        [piece] = call(
            functools.partial(fetch_kernel, layer),
            [((width, part), BF16, ANY_SPEC)],
            (where, expert_in),
            [SMEM_SPEC, ANY_SPEC],
            [pltpu.SemaphoreType.DMA((1,))],
            deps=deps,
        )
        return piece, pair_of(piece)

    def pair_of(piece):
        got = swap(piece, "tensor")
        return got, swap(got, "replica")

    def place_spec(layer):
        return layer_spec((1, slots, rows), layer)

    def gain_spec(layer):
        return layer_spec((1, 2, width), layer)

    def columns(size, shift=0):
        return pl.BlockSpec(size, lambda step: (0, step + shift))

    def lines(size, shift=0):
        return pl.BlockSpec(size, lambda step: (step + shift, 0))

    pack_flops = 2 * slots * rows * width
    weights = [pltpu.VMEM((4, width, part), BF16), pltpu.VMEM((4, part, width), BF16)]
    total = pltpu.VMEM((slots, width), F32)
    dots = pltpu.VMEM((slots, 1), F32)
    sems = pltpu.SemaphoreType.DMA((8,))
    expert_flops = 8 * slots * width * hidden
    rows_out = ((slots, width), BF16)
    hidden_spec = columns((slots, part))
    hidden_out = ((slots, 2 * hidden), BF16, hidden_spec)

    _, whole_in = fetch(0)
    attend_deps = ()
    router_t = jnp.swapaxes(router, 1, 2)
    routes_t = jnp.swapaxes(routes, 1, 2).reshape(layers, 2, images, SEQ)
    routes_t = jnp.pad(
        routes_t, ((0, 0), (0, 0), (0, 0), (0, PAD - SEQ)), constant_values=-1
    ).reshape(layers, 2, rows)
    upstream = spread(cotangent)
    stream_args = (spread(tokens),)
    place = None
    saved = []
    for layer in range(layers):
        h, a, proj, mixed, term = call(
            functools.partial(attend_kernel, layer == 0),
            [
                ((rows, width), F32),
                ((rows, width), BF16),
                ((3, rows, local), BF16),
                ((rows, local), BF16),
                ((rows, width), BF16),
            ],
            (*stream_args, gains, attn_qkv, attn_out),
            [
                *([VMEM_SPEC] * len(stream_args)),
                gain_spec(layer),
                layer_spec((1, 3, width, local), layer),
                layer_spec((1, local, width), layer),
            ],
            flops=8 * rows * width * local + 4 * rows * PAD * local,
            deps=attend_deps,
        )
        if place is None:
            place, send = call(
                functools.partial(place_kernel, slot_half),
                [((layers, slots, rows), BF16), rows_out],
                (where, routes_t, upstream),
                [SMEM_SPEC, VMEM_SPEC, VMEM_SPEC],
                flops=2 * layers * rows * rows * experts + pack_flops,
                deps=(term,),
            )
            received_grad = exchange(send)
        mid, send, piece = call(
            functools.partial(route_kernel, layer),
            [((rows, width), F32), rows_out, ((part, width), BF16, ANY_SPEC)],
            (where, h, term, swap(term, "tensor"), gains, place, expert_out),
            [SMEM_SPEC] + [VMEM_SPEC] * 3 + [gain_spec(layer), place_spec(layer), ANY_SPEC],
            [pltpu.SemaphoreType.DMA((1,))],
            flops=pack_flops,
        )
        whole = (expert_in, *whole_in, expert_out, *pair_of(piece))
        received = exchange(send)
        if layer < last:
            piece, whole_in = fetch(layer + 1, (received,))
            attend_deps = (whole_in[0],)
            reply, act, slope = call(
                functools.partial(expert_kernel, layer),
                [rows_out, hidden_out, hidden_out],
                (where, received, router_t[layer], *whole),
                [SMEM_SPEC, VMEM_SPEC, VMEM_SPEC] + [ANY_SPEC] * 6,
                [*weights, total, sems],
                flops=expert_flops,
                limit=56,
                deps=(piece,),
                grid=(4,),
            )
            returned = exchange(reply)
            [term] = call(
                unpack_kernel,
                [((rows, width), BF16)],
                (place, returned),
                [place_spec(layer), VMEM_SPEC],
                flops=pack_flops,
            )
            stream_args = (mid, term, swap(term, "tensor"))
            saved.append((h, a, proj, mixed, mid, received, act, slope, whole))
        else:
            saved.append((h, a, proj, mixed, mid, received, None, None, whole))

    small = [None] * layers
    sums = [None] * layers
    grad_in = grad_out = mixed_out = None
    finishers = []
    for layer in reversed(range(layers)):
        h, a, proj, mixed, mid, received, act, slope, whole = saved[layer]
        back_outs = [hidden_out, rows_out, ((experts, width), F32)]
        if layer == last:
            reply, back, act, pre_grad, scaled, router_grad = call(
                functools.partial(expert_both_kernel, layer),
                [rows_out, rows_out, hidden_out, *back_outs],
                (where, received_grad, received, router_t[layer], *whole),
                [SMEM_SPEC] + [VMEM_SPEC] * 3 + [ANY_SPEC] * 6,
                [*weights, total, total, dots, sems],
                flops=2 * expert_flops,
                limit=56,
                grid=(4,),
            )
        else:
            back, pre_grad, scaled, router_grad = call(
                functools.partial(expert_back_kernel, layer),
                [rows_out, *back_outs],
                (where, received_grad, received, act, slope, router_t[layer], *whole),
                [SMEM_SPEC, VMEM_SPEC, VMEM_SPEC, hidden_spec, hidden_spec, VMEM_SPEC] + [ANY_SPEC] * 6,
                [*weights, total, dots, sems],
                flops=expert_flops,
                limit=56,
                deps=(far[0], sums[last].split()),
                grid=(4,),
            )
        returned = exchange(back)
        if layer == last:
            term, reply = call(
                unpack_pass_kernel,
                [((rows, width), BF16), (*rows_out, ANY_SPEC)],
                (place, returned, reply),
                [place_spec(layer), VMEM_SPEC, ANY_SPEC],
                [pltpu.SemaphoreType.DMA((1,))],
                flops=pack_flops,
            )
        else:
            [term] = call(
                unpack_kernel,
                [((rows, width), BF16)],
                (place, returned),
                [place_spec(layer), VMEM_SPEC],
                flops=pack_flops,
                deps=(far[1], sums[last].split()),
            )
        got = swap(term, "tensor")
        in_other, out_other = call(
            grad_other_kernel,
            [
                ((half, 2 * hidden), BF16, columns((half, part))),
                ((2 * hidden, half), BF16, lines((part, half))),
            ],
            (where, received, scaled, pre_grad, act),
            [SMEM_SPEC, VMEM_SPEC, VMEM_SPEC, hidden_spec, hidden_spec],
            flops=4 * slots * hidden * width,
            deps=(term,),
            grid=(4,),
        )
        in_got, out_got = swap(in_other, "replica"), swap(out_other, "replica")
        upstream, gain_two, term, *weight_grads = call(
            attend_back_kernel,
            [
                ((rows, width), F32),
                ((1, width), F32),
                ((rows, width), BF16),
                *[((2 * width, local), BF16)] * 2,
            ],
            (where, term, got, mid, gains, upstream, a, proj, mixed, attn_qkv, attn_out),
            [SMEM_SPEC]
            + [VMEM_SPEC] * 3
            + [gain_spec(layer)]
            + [VMEM_SPEC] * 4
            + [layer_spec((1, 3, width, local), layer), layer_spec((1, local, width), layer)],
            [pltpu.VMEM((3, rows, local), BF16), pltpu.VMEM((rows, local), BF16)],
            flops=16 * rows * width * local + 10 * rows * PAD * local,
            deps=(in_other, out_other) if layer == last else (in_other, out_other, sums[last].finish()),
        )
        if layer == last:
            [done] = call(
                unpack_kernel,
                [((rows, width), BF16)],
                (place, exchange(reply)),
                [place_spec(layer), VMEM_SPEC],
                flops=pack_flops,
            )
            done = done.astype(F32) + swap(done, "tensor").astype(F32)
            mixed_out = gathered((mid + done).astype(BF16))

        mine, other = weight_grads
        sums[layer] = ExpertSum(mine, swap(other, "replica"), experts)
        got = swap(term, "tensor")
        in_far, out_far = call(
            grad_far_kernel,
            [
                ((half, hidden), BF16, columns((half, part))),
                ((hidden, half), BF16, lines((part, half))),
            ],
            (where, received, scaled, pre_grad, act, in_got, out_got),
            [
                SMEM_SPEC,
                VMEM_SPEC,
                VMEM_SPEC,
                columns((slots, part), 2),
                columns((slots, part), 2),
                columns((half, part), 2),
                lines((part, half), 2),
            ],
            flops=2 * slots * hidden * width,
            deps=(term,),
            grid=(2,),
        )
        if layer > 0:
            upstream, gain_one, send = call(
                functools.partial(stream_back_kernel, True),
                [((rows, width), F32), ((1, width), F32), rows_out],
                (term, got, h, gains, upstream, place),
                [VMEM_SPEC] * 3 + [gain_spec(layer), VMEM_SPEC, place_spec(layer - 1)],
                flops=pack_flops,
                deps=(in_far, out_far, sums[last].split()),
            )
            received_grad = exchange(send)
        else:
            upstream, gain_one = call(
                functools.partial(stream_back_kernel, False),
                [((rows, width), F32), ((1, width), F32)],
                (term, got, h, gains, upstream),
                [VMEM_SPEC] * 3 + [gain_spec(layer), VMEM_SPEC],
                deps=(in_far, out_far, sums[last].join()),
            )
        in_far, out_far = far = swap(in_far, "tensor"), swap(out_far, "tensor")
        gain_pair = jnp.where(side == 0, jnp.concatenate([gain_one, gain_two]), 0.0)
        small[layer] = jnp.concatenate([router_grad, gain_pair])

        def finish_own(deps, layer=layer, args=(where, received, scaled, pre_grad, act, in_got, out_got, in_far, out_far)):
            nonlocal grad_in, grad_out
            stacked = () if grad_in is None else (grad_in, grad_out)
            grad_in, grad_out = call(
                grad_own_kernel,
                [
                    (
                        (layers, half, hidden),
                        F32,
                        pl.BlockSpec((1, half, part), lambda step: (layer, 0, step)),
                    ),
                    (
                        (layers, hidden, half),
                        F32,
                        pl.BlockSpec((1, part, half), lambda step: (layer, step, 0)),
                    ),
                ],
                (*args, *stacked),
                [
                    SMEM_SPEC,
                    VMEM_SPEC,
                    VMEM_SPEC,
                    hidden_spec,
                    hidden_spec,
                    columns((half, part)),
                    lines((part, half)),
                    columns((half, part)),
                    lines((part, half)),
                    *([ANY_SPEC] * len(stacked)),
                ],
                flops=2 * slots * hidden * width,
                deps=deps,
                grid=(2,),
                alias={9: 0, 10: 1} if stacked else None,
            )

        finishers.append(finish_own)

    finishers[0]((term,))
    finishers[1]((upstream,))

    grad_qkv, grad_proj = [], []
    for layer in range(layers):
        if layer < last:
            sums[layer].finish(far[:1])
            sums[layer].join(far[1:])
        mine = sums[layer].result()
        got = swap(mine, "replica")
        lower = jnp.where(core == 0, mine, got).astype(F32)
        upper = jnp.where(core == 0, got, mine).astype(F32)
        grad_qkv.append(jnp.concatenate([lower, upper[:width]]).reshape(3, width, local))
        grad_proj.append(
            jnp.concatenate([upper[width : width + local], upper[width + local :]], axis=1)
        )
    small = sum_all(jnp.stack(small))
    return (
        mixed_out,
        gathered(upstream),
        small[:, experts:],
        jnp.stack(grad_qkv),
        jnp.stack(grad_proj),
        jnp.swapaxes(small[:, :experts], 1, 2),
        grad_in[:, None],
        grad_out[:, None],
    )


def solution(mesh):
    return jax.shard_map(
        on_device,
        mesh=mesh,
        in_specs=(
            P(("expert", "replica"), None),
            P(),
            P(None, None, None, "tensor"),
            P(None, "tensor", None),
            P(),
            P(None, "expert", None, "tensor"),
            P(None, "expert", "tensor", None),
            P(None, ("expert", "replica"), None),
            P(("expert", "replica"), None),
        ),
        out_specs=(
            P(("expert", "replica"), None),
            P(("expert", "replica"), None),
            P(),
            P(None, None, None, "tensor"),
            P(None, "tensor", None),
            P(),
            P(None, "expert", "replica", "tensor"),
            P(None, "expert", "tensor", "replica"),
        ),
        check_vma=False,
    )
```

```python
import functools

import jax
import jax.numpy as jnp
from jax import lax
from jax.experimental import pallas as pl
from jax.experimental.pallas import tpu as pltpu
from jax.sharding import PartitionSpec as P

HEAD_DIM = 64
SEQ = 197
PAD = 208
PAIR = 2 * HEAD_DIM
EPSILON = 1e-06
GELU_A = 0.7978845608028654
GELU_B = 0.044715
F32 = jnp.float32
BF16 = jnp.bfloat16
NT = (((1,), (1,)), ((), ()))
TN = (((0,), (0,)), ((), ()))


def mm(a, b):
    return jnp.dot(a, b, preferred_element_type=F32)


def mm_nt(a, b):
    return lax.dot_general(a, b, NT, preferred_element_type=F32)


def mm_tn(a, b):
    return lax.dot_general(a, b, TN, preferred_element_type=F32)


def normalize(stream):
    shifted = stream - jnp.mean(stream, axis=-1, keepdims=True)
    scale = lax.rsqrt(jnp.mean(shifted * shifted, axis=-1, keepdims=True) + EPSILON)
    return shifted * scale, scale


def norm_back(stream, gain, out_grad):
    xhat, scale = normalize(stream)
    u = out_grad * gain
    mean_u = jnp.mean(u, axis=-1, keepdims=True)
    mean_ux = jnp.mean(u * xhat, axis=-1, keepdims=True)
    return scale * (u - mean_u - xhat * mean_ux), jnp.sum(out_grad * xhat, axis=0, keepdims=True)


def both(own_ref, got_ref):
    return own_ref[...].astype(F32) + got_ref[...].astype(F32)


VMEM_SPEC = pl.BlockSpec(memory_space=pltpu.VMEM)
SMEM_SPEC = pl.BlockSpec(memory_space=pltpu.SMEM)
ANY_SPEC = pl.BlockSpec(memory_space=pl.ANY)


def call(body, outs, args, specs, scratch=(), micros=1.5, limit=40, deps=(), grid=(1,), alias=None):
    out_specs = [o[2] if len(o) > 2 else VMEM_SPEC for o in outs]
    outs = [jax.ShapeDtypeStruct(o[0], o[1]) for o in outs]
    taken, last = len(args), len(args) + len(deps)

    def kernel(*refs):
        body(*refs[:taken], *refs[last:])

    return pl.pallas_call(
        kernel,
        grid=grid,
        out_shape=outs,
        in_specs=[*specs, *([ANY_SPEC] * len(deps))],
        out_specs=out_specs,
        scratch_shapes=list(scratch),
        input_output_aliases=alias or {},
        compiler_params=pltpu.CompilerParams(vmem_limit_bytes=limit << 20),
        cost_estimate=pl.CostEstimate(flops=1, bytes_accessed=int(micros * 1.8e6), transcendentals=0),
    )(*args, *deps)


def layer_spec(shape, layer):
    return pl.BlockSpec(shape, lambda step: (layer,) + (0,) * (len(shape) - 1))


def place_kernel(slot_half, where_ref, routes_ref, rows_ref, place_ref, send_ref):
    layers, _, rows = routes_ref.shape
    experts = place_ref.shape[1] // slot_half
    first = where_ref[0] * slot_half
    before_of = lax.broadcasted_iota(jnp.int32, (rows, rows), 0) < lax.broadcasted_iota(
        jnp.int32, (rows, rows), 1
    )
    earlier = jnp.where(before_of, 1.0, 0.0).astype(BF16)
    labels = lax.broadcasted_iota(jnp.int32, (experts, rows), 0)
    slots = lax.broadcasted_iota(jnp.int32, (slot_half, rows), 0)
    for layer in range(layers):
        named = (labels == routes_ref[layer, 0:1, :]) | (labels == routes_ref[layer, 1:2, :])
        count = mm(jnp.where(named, 1.0, 0.0).astype(BF16), earlier)
        slot = jnp.where(named, count.astype(jnp.int32) - first, -1)
        for e in range(experts):
            hit = slots == slot[e : e + 1, :]
            place_ref[layer, e * slot_half : (e + 1) * slot_half, :] = jnp.where(
                hit, 1.0, 0.0
            ).astype(BF16)
    send_ref[...] = mm(place_ref[layers - 1], rows_ref[...]).astype(BF16)


def piece_of(matrix_in, matrix_out, layer, core):
    if matrix_in is not None:
        part = matrix_in.shape[3] // 2
        return matrix_in.at[layer, 0, :, pl.ds(pl.multiple_of(core * part, part), part)]
    part = matrix_out.shape[2] // 2
    return matrix_out.at[layer, 0, pl.ds(pl.multiple_of(core * part, part), part), :]


def fetch_kernel(layer, where_ref, source_ref, piece_ref, sem):
    copy = pltpu.make_async_copy(
        piece_of(source_ref, None, layer, where_ref[2]), piece_ref, sem.at[0]
    )
    copy.start()
    copy.wait()


def unpack_kernel(place_ref, got_ref, out_ref):
    out_ref[...] = mm_tn(place_ref[0], got_ref[...]).astype(BF16)


def unpack_pass_kernel(place_ref, got_ref, reply_ref, out_ref, passed_ref, sem):
    copy = pltpu.make_async_copy(reply_ref, passed_ref, sem.at[0])
    copy.start()
    out_ref[...] = mm_tn(place_ref[0], got_ref[...]).astype(BF16)
    copy.wait()


def pair_masks():
    lane = lax.broadcasted_iota(jnp.int32, (PAD, PAIR), 1)
    return lane < HEAD_DIM


def softmax_rows(q, k):
    scores = mm_nt(q, k) * HEAD_DIM ** (-0.5)
    column = lax.broadcasted_iota(jnp.int32, scores.shape, 1)
    scores = jnp.where(column < SEQ, scores, -1e30)
    top = jnp.max(scores, axis=-1, keepdims=True)
    weights = jnp.exp(scores - top)
    return weights / jnp.sum(weights, axis=-1, keepdims=True)


def attend_kernel(first, *refs):
    if first:
        tokens_ref, gain_ref, qkv_ref, wo_ref, h_ref, a_ref, proj_ref, mixed_ref, out_ref = refs
        h = tokens_ref[...].astype(F32)
    else:
        mid_ref, own_ref, got_ref, gain_ref, qkv_ref, wo_ref = refs[:6]
        h_ref, a_ref, proj_ref, mixed_ref, out_ref = refs[6:]
        h = mid_ref[...] + both(own_ref, got_ref)
    h_ref[...] = h
    a = (normalize(h)[0] * gain_ref[0, 0:1, :]).astype(BF16)
    a_ref[...] = a
    for c in range(3):
        proj_ref[c] = mm(a, qkv_ref[0, c]).astype(BF16)
    low = pair_masks()
    zero = jnp.zeros((PAD, PAIR), BF16)
    for image in range(a.shape[0] // PAD):
        rows = slice(image * PAD, (image + 1) * PAD)
        for pair in range(proj_ref.shape[2] // PAIR):
            lanes = slice(pair * PAIR, (pair + 1) * PAIR)
            q, k, v = (proj_ref[c, rows, lanes] for c in range(3))
            p0 = softmax_rows(jnp.where(low, q, zero), k).astype(BF16)
            p1 = softmax_rows(jnp.where(low, zero, q), k).astype(BF16)
            mixed_ref[rows, lanes] = jnp.where(low, mm(p0, v), mm(p1, v)).astype(BF16)
    out_ref[...] = mm(mixed_ref[...], wo_ref[0]).astype(BF16)


def route_kernel(
    layer, where_ref, h_ref, own_ref, got_ref, gain_ref, place_ref, source_ref, mid_ref, send_ref, piece_ref, sem
):
    copy = pltpu.make_async_copy(
        piece_of(None, source_ref, layer, where_ref[2]), piece_ref, sem.at[0]
    )
    copy.start()
    mid = h_ref[...] + both(own_ref, got_ref)
    mid_ref[...] = mid
    z = (normalize(mid)[0] * gain_ref[0, 1:2, :]).astype(BF16)
    send_ref[...] = mm(place_ref[0], z).astype(BF16)
    copy.wait()


def load_weights(layer, core, sources, win, wout, sems, in_first):
    win_own, win_a, win_b, wout_own, wout_a, wout_b = sources
    part = win.shape[2]
    groups = []
    for c in range(2):
        groups.append(
            [
                (win_own.at[layer, 0, :, pl.ds(c * part, part)], win.at[c], 2 * c),
                (wout_own.at[layer, 0, pl.ds(c * part, part), :], wout.at[c], 2 * c + 1),
            ]
        )
    groups.append(
        [
            (win_a, win.at[2 + core], 4),
            (wout_a, wout.at[2 + core], 5),
            (win_b, win.at[3 - core], 6),
            (wout_b, wout.at[3 - core], 7),
        ]
    )
    groups = [[pltpu.make_async_copy(s, d, sems.at[i]) for s, d, i in group] for group in groups]

    @pl.when(pl.program_id(0) == 0)
    def _():
        for group in groups:
            for copy in group:
                copy.start()

    for step, group in enumerate(groups):

        @pl.when(pl.program_id(0) == step)
        def _(group=group):
            for copy in group:
                copy.wait()


def gate_of(x, router, expert):
    logits = mm_nt(x, router)
    gate = jnp.exp(logits - jnp.max(logits, axis=-1, keepdims=True))
    gate = gate / jnp.sum(gate, axis=-1, keepdims=True)
    mine = lax.broadcasted_iota(jnp.int32, gate.shape, 1) == expert
    return gate, mine, jnp.sum(jnp.where(mine, gate, 0.0), axis=-1, keepdims=True)


def bend(pre):
    square = pre * pre
    bent = jnp.tanh(pre * (GELU_A + (GELU_A * GELU_B) * square))
    half = 0.5 + 0.5 * bent
    slope = half + pre * (1.0 - bent * bent) * (0.5 * GELU_A + (1.5 * GELU_A * GELU_B) * square)
    return pre * half, slope


def add_step(total, term):
    @pl.when(pl.program_id(0) == 0)
    def _():
        total[...] = term

    @pl.when(pl.program_id(0) > 0)
    def _():
        total[...] += term


def expert_kernel(
    layer, where_ref, x_ref, router_ref, win_own, win_a, win_b, wout_own, wout_a, wout_b,
    out_ref, act_ref, slope_ref, win, wout, total, sems,
):
    step = pl.program_id(0)
    sources = (win_own, win_a, win_b, wout_own, wout_a, wout_b)
    load_weights(layer, where_ref[2], sources, win, wout, sems, True)
    act, slope = bend(mm(x_ref[...], win[step]))
    act = act.astype(BF16)
    act_ref[...] = act
    slope_ref[...] = slope.astype(BF16)
    add_step(total, mm(act, wout[step]))

    @pl.when(step == pl.num_programs(0) - 1)
    def _():
        _, _, share = gate_of(x_ref[...], router_ref[...], where_ref[1])
        out_ref[...] = (share * total[...]).astype(BF16)


def finish_back(x_ref, router_ref, gate, mine, share, dot, total, out_ref, router_grad_ref):
    logit_grad = (dot * share * (jnp.where(mine, 1.0, 0.0) - gate)).astype(BF16)
    router_grad_ref[...] = mm_tn(logit_grad, x_ref[...])
    out_ref[...] = (total + mm(logit_grad, router_ref[...])).astype(BF16)


def expert_back_kernel(
    layer, where_ref, g_ref, x_ref, act_ref, slope_ref, router_ref,
    win_own, win_a, win_b, wout_own, wout_a, wout_b,
    out_ref, pre_grad_ref, scaled_ref, router_grad_ref, win, wout, total, dot_ref, sems,
):
    step = pl.program_id(0)
    sources = (win_own, win_a, win_b, wout_own, wout_a, wout_b)
    load_weights(layer, where_ref[2], sources, win, wout, sems, False)
    g = g_ref[...]
    gate, mine, share = gate_of(x_ref[...], router_ref[...], where_ref[1])
    u = mm_nt(g, wout[step])
    pre_grad = (share * u * slope_ref[...].astype(F32)).astype(BF16)
    pre_grad_ref[...] = pre_grad
    add_step(total, mm_nt(pre_grad, win[step]))
    add_step(dot_ref, jnp.sum(u * act_ref[...].astype(F32), axis=-1, keepdims=True))

    @pl.when(step == pl.num_programs(0) - 1)
    def _():
        scaled_ref[...] = (share * g.astype(F32)).astype(BF16)
        finish_back(
            x_ref, router_ref, gate, mine, share, dot_ref[...], total[...], out_ref, router_grad_ref
        )


def expert_both_kernel(
    layer, where_ref, g_ref, x_ref, router_ref,
    win_own, win_a, win_b, wout_own, wout_a, wout_b,
    out_ref, back_ref, act_ref, pre_grad_ref, scaled_ref, router_grad_ref,
    win, wout, total, back_total, dot_ref, sems,
):
    step = pl.program_id(0)
    sources = (win_own, win_a, win_b, wout_own, wout_a, wout_b)
    load_weights(layer, where_ref[2], sources, win, wout, sems, True)
    g = g_ref[...]
    gate, mine, share = gate_of(x_ref[...], router_ref[...], where_ref[1])
    act, slope = bend(mm(x_ref[...], win[step]))
    u = mm_nt(g, wout[step])
    act = act.astype(BF16)
    act_ref[...] = act
    pre_grad = (share * u * slope).astype(BF16)
    pre_grad_ref[...] = pre_grad
    add_step(total, mm(act, wout[step]))
    add_step(back_total, mm_nt(pre_grad, win[step]))
    add_step(dot_ref, jnp.sum(u * act.astype(F32), axis=-1, keepdims=True))

    @pl.when(step == pl.num_programs(0) - 1)
    def _():
        out_ref[...] = (share * total[...]).astype(BF16)
        scaled_ref[...] = (share * g.astype(F32)).astype(BF16)
        finish_back(
            x_ref, router_ref, gate, mine, share, dot_ref[...], back_total[...], back_ref, router_grad_ref
        )


def half_of(ref, which):
    half = ref.shape[1] // 2
    return ref[:, pl.ds(pl.multiple_of(which * half, half), half)]


def grad_other_kernel(where_ref, x_ref, scaled_ref, pre_grad_ref, act_ref, in_ref, out_ref):
    other = 1 - where_ref[2]
    in_ref[...] = mm_tn(half_of(x_ref, other), pre_grad_ref[...]).astype(BF16)
    out_ref[...] = mm_tn(act_ref[...], half_of(scaled_ref, other)).astype(BF16)


def grad_far_kernel(
    where_ref, x_ref, scaled_ref, pre_grad_ref, act_ref, in_got_ref, out_got_ref, in_ref, out_ref
):
    core = where_ref[2]
    term = mm_tn(half_of(x_ref, core), pre_grad_ref[...])
    in_ref[...] = (term + in_got_ref[...].astype(F32)).astype(BF16)
    term = mm_tn(act_ref[...], half_of(scaled_ref, core))
    out_ref[...] = (term + out_got_ref[...].astype(F32)).astype(BF16)


def grad_own_kernel(
    where_ref, x_ref, scaled_ref, pre_grad_ref, act_ref, in_got_ref, out_got_ref, in_far_ref, out_far_ref, *refs
):
    core = where_ref[2]
    in_ref, out_ref = refs[-2:]
    term = mm_tn(half_of(x_ref, core), pre_grad_ref[...])
    in_ref[0] = term + in_got_ref[...].astype(F32) + in_far_ref[...].astype(F32)
    term = mm_tn(act_ref[...], half_of(scaled_ref, core))
    out_ref[0] = term + out_got_ref[...].astype(F32) + out_far_ref[...].astype(F32)


def attend_back_kernel(
    where_ref, own_ref, got_ref, mid_ref, gain_ref, g_ref, a_ref, proj_ref, mixed_ref, qkv_ref, wo_ref,
    g_out_ref, gain_grad_ref, out_ref, *refs,
):
    back_ref, mixed_grad_ref = refs[-2:]
    h_grad, gain_grad_ref[...] = norm_back(
        mid_ref[...], gain_ref[0, 1:2, :], both(own_ref, got_ref)
    )
    g = g_ref[...].astype(F32) + h_grad
    g_out_ref[...] = g
    out_grad = g.astype(BF16)
    width = proj_ref.shape[2]
    depth = a_ref.shape[1]
    mixed_grad_ref[...] = mm_nt(out_grad, wo_ref[0]).astype(BF16)
    low = pair_masks()
    zero = jnp.zeros((PAD, PAIR), BF16)
    for image in range(g.shape[0] // PAD):
        rows = slice(image * PAD, (image + 1) * PAD)
        for pair in range(width // PAIR):
            lanes = slice(pair * PAIR, (pair + 1) * PAIR)
            q, k, v = (proj_ref[c, rows, lanes] for c in range(3))
            dm = mixed_grad_ref[rows, lanes]
            parts = []
            for side in range(2):
                def pick(t, side=side):
                    return jnp.where(low, t, zero) if side == 0 else jnp.where(low, zero, t)

                probs = softmax_rows(pick(q), k)
                prob_grad = mm_nt(pick(dm), v)
                row = jnp.sum(prob_grad * probs, axis=-1, keepdims=True)
                score_grad = (probs * (prob_grad - row)).astype(BF16)
                parts.append(
                    (
                        mm(score_grad, k) * HEAD_DIM ** (-0.5),
                        mm_tn(score_grad, q) * HEAD_DIM ** (-0.5),
                        mm_tn(probs.astype(BF16), dm),
                    )
                )
            for c in range(3):
                back_ref[c, rows, lanes] = jnp.where(low, parts[0][c], parts[1][c]).astype(BF16)
    total = mm_nt(back_ref[0], qkv_ref[0, 0])
    total += mm_nt(back_ref[1], qkv_ref[0, 1])
    total += mm_nt(back_ref[2], qkv_ref[0, 2])
    out_ref[...] = total.astype(BF16)
    core = where_ref[2]

    def put(block, start, value):
        @pl.when(core == block // 2)
        def _():
            refs[0][start : start + value.shape[0], :] = value.astype(BF16)

        @pl.when(core != block // 2)
        def _():
            refs[1][start : start + value.shape[0], :] = value.astype(BF16)

    for c in range(3):
        put(c, c % 2 * depth, mm_tn(a_ref[...], back_ref[c]))
    proj_grad = mm_tn(mixed_ref[...], out_grad)
    for c in range(depth // width):
        put(3, depth + c * width, proj_grad[:, c * width : (c + 1) * width])


def stream_back_kernel(pack, *refs):
    if pack:
        own_ref, got_ref, h_ref, gain_ref, g_ref, place_ref, g_out_ref, gain_grad_ref, send_ref = refs
    else:
        own_ref, got_ref, h_ref, gain_ref, g_ref, g_out_ref, gain_grad_ref = refs
    h_grad, gain_grad_ref[...] = norm_back(h_ref[...], gain_ref[0, 0:1, :], both(own_ref, got_ref))
    g = g_ref[...] + h_grad
    if not pack:
        for image in range(g.shape[0] // PAD):
            g_out_ref[image * SEQ : (image + 1) * SEQ, :] = g[image * PAD : image * PAD + SEQ, :]
    if pack:
        g_out_ref[...] = g
        send_ref[...] = mm(place_ref[0], g.astype(BF16)).astype(BF16)


def swap(value, axis):
    return lax.ppermute(value, axis, [(0, 1), (1, 0)])


def partner(value, axis, bit):
    count = lax.axis_size(axis)
    return lax.ppermute(value, axis, [(i, i ^ (1 << bit)) for i in range(count)])


def first_split_kernel(sides_ref, mine_ref, got_ref, *outs):
    for i in range(2):
        out_ref, send_ref = outs[2 * i], outs[2 * i + 1]
        half = out_ref.shape[0]
        side = sides_ref[i]
        mine, other = pl.ds(side * half, half), pl.ds((1 - side) * half, half)
        out_ref[...] = mine_ref[i, mine].astype(F32) + got_ref[i, mine].astype(F32)
        send_ref[...] = (mine_ref[i, other].astype(F32) + got_ref[i, other].astype(F32)).astype(BF16)


def last_join_kernel(sides_ref, own_a_ref, got_a_ref, own_b_ref, got_b_ref, out_ref):
    for i, (own_ref, got_ref) in enumerate(((own_a_ref, got_a_ref), (own_b_ref, got_b_ref))):
        half = own_ref.shape[0]
        side = sides_ref[i]
        out_ref[i, pl.ds(side * half, half)] = own_ref[...]
        out_ref[i, pl.ds((1 - side) * half, half)] = got_ref[...]


def layout_kernel(where_ref, mine_ref, got_ref, *refs):
    qkv_ref, proj_ref = refs[-2:]
    depth, width = qkv_ref.shape[2:]

    def write(low_ref, high_ref):
        qkv_ref[0, 0] = low_ref[0].astype(F32)
        qkv_ref[0, 1] = low_ref[1].astype(F32)
        qkv_ref[0, 2] = high_ref[0].astype(F32)
        for c in range(depth // width):
            rows = slice(c * width, (c + 1) * width)
            proj_ref[0, :, rows] = high_ref[1, rows, :].astype(F32)

    @pl.when(where_ref[2] == 0)
    def _():
        write(mine_ref, got_ref)

    @pl.when(where_ref[2] == 1)
    def _():
        write(got_ref, mine_ref)


def split_kernel(sides_ref, keep_a_ref, got_a_ref, keep_b_ref, got_b_ref, *outs):
    for i, (keep_ref, got_ref) in enumerate(((keep_a_ref, got_a_ref), (keep_b_ref, got_b_ref))):
        out_ref, send_ref = outs[2 * i], outs[2 * i + 1]
        half = out_ref.shape[0]
        side = sides_ref[i]
        mine, other = pl.ds(side * half, half), pl.ds((1 - side) * half, half)
        out_ref[...] = keep_ref[mine].astype(F32) + got_ref[mine].astype(F32)
        send_ref[...] = (keep_ref[other].astype(F32) + got_ref[other].astype(F32)).astype(BF16)


def last_sum_kernel(keep_a_ref, got_a_ref, keep_b_ref, got_b_ref, a_ref, b_ref):
    a_ref[...] = both(keep_a_ref, got_a_ref).astype(BF16)
    b_ref[...] = both(keep_b_ref, got_b_ref).astype(BF16)


def join_kernel(sides_ref, own_a_ref, got_a_ref, own_b_ref, got_b_ref, a_ref, b_ref):
    pairs = ((own_a_ref, got_a_ref, a_ref), (own_b_ref, got_b_ref, b_ref))
    for i, (own_ref, got_ref, out_ref) in enumerate(pairs):
        half = own_ref.shape[0]
        side = sides_ref[i]
        out_ref[pl.ds(side * half, half)] = own_ref[...]
        out_ref[pl.ds((1 - side) * half, half)] = got_ref[...]


class ExpertSum:
    def __init__(self, mine, got, experts):
        rows, width = mine.shape
        block = rows // (2 * experts)
        mine, got = (v.reshape(2, experts, block, width) for v in (mine, got))
        bits = list(range(experts.bit_length() - 1))
        self.orders = list(zip(bits, [*bits[1::-1], *bits[2:]]))
        me = lax.axis_index("expert")
        self.sides = [jnp.stack([(me >> a) & 1, (me >> b) & 1]).astype(jnp.int32) for a, b in self.orders]
        self.state = (mine, got)
        self.count, self.block, self.width = experts, block, width
        self.step = 0

    def shape(self):
        return (self.count, self.block, self.width)

    def split(self, deps=()):
        self.count //= 2
        a, b = self.orders[self.step]
        keep_a, send_a, keep_b, send_b = call(
            first_split_kernel if self.step == 0 else split_kernel,
            [(self.shape(), F32), (self.shape(), BF16)] * 2,
            (self.sides[self.step], *self.state),
            [SMEM_SPEC] + [VMEM_SPEC] * len(self.state),
            deps=deps,
        )
        self.step += 1
        self.state = (keep_a, partner(send_a, "expert", a), keep_b, partner(send_b, "expert", b))
        return send_a

    def finish(self, deps=()):
        while self.step < len(self.orders):
            self.split()
        self.state = call(
            last_sum_kernel, [(self.shape(), BF16)] * 2, self.state, [VMEM_SPEC] * 4, deps=deps
        )
        return self.state[0]

    def join(self, deps=()):
        self.step -= 1
        own_a, own_b = self.state
        a, b = self.orders[self.step]
        got_a, got_b = partner(own_a, "expert", a), partner(own_b, "expert", b)
        self.count *= 2
        self.state = call(
            join_kernel if self.step else last_join_kernel,
            [(self.shape(), BF16)] * 2 if self.step else [((2, *self.shape()), BF16)],
            (self.sides[self.step], own_a, got_a, own_b, got_b),
            [SMEM_SPEC] + [VMEM_SPEC] * 4,
            deps=deps,
        )
        return self.state[0]

    def result(self):
        while self.step:
            self.join()
        return self.state[0].reshape(2, -1, self.width)


def sum_small(value):
    value = value + swap(value, "replica")
    for bit in range(lax.axis_size("expert").bit_length() - 1):
        value = value + partner(value, "expert", bit)
    return value


def on_device(tokens, gains, attn_qkv, attn_out, router, expert_in, expert_out, routes, cotangent):
    row_count, width = tokens.shape
    layers = attn_qkv.shape[0]
    local = attn_qkv.shape[3]
    images = row_count // SEQ
    rows = images * PAD
    experts = router.shape[2]
    hidden = expert_in.shape[3]
    part = hidden // 2
    half = width // 2
    capacity = 8 * (5 * row_count // (16 * experts) + 1)
    slot_half = capacity // 2
    slots = experts * slot_half
    side = lax.axis_index("tensor")
    core = lax.axis_index("replica")
    where = jnp.stack([side, lax.axis_index("expert"), core]).astype(jnp.int32)
    last = layers - 1

    def spread(array):
        array = array.reshape(images, SEQ, width)
        return jnp.pad(array, ((0, 0), (0, PAD - SEQ), (0, 0))).reshape(rows, width)

    def gathered(array):
        return array.reshape(images, PAD, width)[:, :SEQ].reshape(row_count, width)

    def exchange(block):
        block = block.reshape(experts, slot_half, width)
        return lax.all_to_all(block, "expert", 0, 0, tiled=True).reshape(slots, width)

    def fetch(layer, deps=()):
        [piece] = call(
            functools.partial(fetch_kernel, layer),
            [((width, part), BF16, ANY_SPEC)],
            (where, expert_in),
            [SMEM_SPEC, ANY_SPEC],
            [pltpu.SemaphoreType.DMA((1,))],
            deps=deps,
        )
        return piece, pair_of(piece)

    def pair_of(piece):
        got = swap(piece, "tensor")
        return got, swap(got, "replica")

    def place_spec(layer):
        return layer_spec((1, slots, rows), layer)

    def gain_spec(layer):
        return layer_spec((1, 2, width), layer)

    def columns(size, shift=0):
        return pl.BlockSpec(size, lambda step: (0, step + shift))

    def lines(size, shift=0):
        return pl.BlockSpec(size, lambda step: (step + shift, 0))

    weights = [pltpu.VMEM((4, width, part), BF16), pltpu.VMEM((4, part, width), BF16)]
    total = pltpu.VMEM((slots, width), F32)
    dots = pltpu.VMEM((slots, 1), F32)
    sems = pltpu.SemaphoreType.DMA((8,))
    rows_out = ((slots, width), BF16)
    hidden_spec = columns((slots, part))
    hidden_out = ((slots, 2 * hidden), BF16, hidden_spec)

    _, whole_in = fetch(0)
    attend_deps = ()
    router_t = jnp.swapaxes(router, 1, 2)
    routes_t = jnp.swapaxes(routes, 1, 2).reshape(layers, 2, images, SEQ)
    routes_t = jnp.pad(
        routes_t, ((0, 0), (0, 0), (0, 0), (0, PAD - SEQ)), constant_values=-1
    ).reshape(layers, 2, rows)
    upstream = spread(cotangent)
    stream_args = (spread(tokens),)
    place = None
    saved = []
    for layer in range(layers):
        h, a, proj, mixed, term = call(
            functools.partial(attend_kernel, layer == 0),
            [
                ((rows, width), F32),
                ((rows, width), BF16),
                ((3, rows, local), BF16),
                ((rows, local), BF16),
                ((rows, width), BF16),
            ],
            (*stream_args, gains, attn_qkv, attn_out),
            [
                *([VMEM_SPEC] * len(stream_args)),
                gain_spec(layer),
                layer_spec((1, 3, width, local), layer),
                layer_spec((1, local, width), layer),
            ],
            micros=5,
            deps=attend_deps,
        )
        if place is None:
            place, send = call(
                functools.partial(place_kernel, slot_half),
                [((layers, slots, rows), BF16), rows_out],
                (where, routes_t, upstream),
                [SMEM_SPEC, VMEM_SPEC, VMEM_SPEC],
                micros=1.5,
                deps=(term,),
            )
            received_grad = exchange(send)
        mid, send, piece = call(
            functools.partial(route_kernel, layer),
            [((rows, width), F32), rows_out, ((part, width), BF16, ANY_SPEC)],
            (where, h, term, swap(term, "tensor"), gains, place, expert_out),
            [SMEM_SPEC] + [VMEM_SPEC] * 3 + [gain_spec(layer), place_spec(layer), ANY_SPEC],
            [pltpu.SemaphoreType.DMA((1,))],
            micros=2,
        )
        whole = (expert_in, *whole_in, expert_out, *pair_of(piece))
        received = exchange(send)
        if layer < last:
            piece, whole_in = fetch(layer + 1, (received,))
            attend_deps = (whole_in[0],)
            reply, act, slope = call(
                functools.partial(expert_kernel, layer),
                [rows_out, hidden_out, hidden_out],
                (where, received, router_t[layer], *whole),
                [SMEM_SPEC, VMEM_SPEC, VMEM_SPEC] + [ANY_SPEC] * 6,
                [*weights, total, sems],
                micros=13,
                limit=56,
                deps=(piece,),
                grid=(4,),
            )
            returned = exchange(reply)
            [term] = call(
                unpack_kernel,
                [((rows, width), BF16)],
                (place, returned),
                [place_spec(layer), VMEM_SPEC],
                micros=2,
            )
            stream_args = (mid, term, swap(term, "tensor"))
            saved.append((h, a, proj, mixed, mid, received, act, slope, whole))
        else:
            saved.append((h, a, proj, mixed, mid, received, None, None, whole))

    small, router_grads = [], []
    sums = [None] * layers
    grad_in = grad_out = None
    finishers = []
    for layer in reversed(range(layers)):
        h, a, proj, mixed, mid, received, act, slope, whole = saved[layer]
        back_outs = [hidden_out, rows_out, ((experts, width), F32)]
        if layer == last:
            reply, back, act, pre_grad, scaled, router_grad = call(
                functools.partial(expert_both_kernel, layer),
                [rows_out, rows_out, hidden_out, *back_outs],
                (where, received_grad, received, router_t[layer], *whole),
                [SMEM_SPEC] + [VMEM_SPEC] * 3 + [ANY_SPEC] * 6,
                [*weights, total, total, dots, sems],
                micros=22,
                limit=56,
                grid=(4,),
            )
        else:
            back, pre_grad, scaled, router_grad = call(
                functools.partial(expert_back_kernel, layer),
                [rows_out, *back_outs],
                (where, received_grad, received, act, slope, router_t[layer], *whole),
                [SMEM_SPEC, VMEM_SPEC, VMEM_SPEC, hidden_spec, hidden_spec, VMEM_SPEC] + [ANY_SPEC] * 6,
                [*weights, total, dots, sems],
                micros=13,
                limit=56,
                deps=(far[0], sums[last].split()),
                grid=(4,),
            )
        returned = exchange(back)
        router_grads.append(router_grad)
        if layer == 0:
            router_all = jnp.concatenate(router_grads)
            router_all = router_all + swap(router_all, "tensor")
        if layer == last:
            term, reply = call(
                unpack_pass_kernel,
                [((rows, width), BF16), (*rows_out, ANY_SPEC)],
                (place, returned, reply),
                [place_spec(layer), VMEM_SPEC, ANY_SPEC],
                [pltpu.SemaphoreType.DMA((1,))],
                micros=2,
            )
        else:
            [term] = call(
                unpack_kernel,
                [((rows, width), BF16)],
                (place, returned),
                [place_spec(layer), VMEM_SPEC],
                micros=2,
                deps=(far[1], sums[last].finish(), router_all),
            )
            finishers[0]((term,))
            reply = exchange(reply)
        got = swap(term, "tensor")
        def other_core(dep):
            in_other, out_other = call(
                grad_other_kernel,
                [
                    ((half, 2 * hidden), BF16, columns((half, part))),
                    ((2 * hidden, half), BF16, lines((part, half))),
                ],
                (where, received, scaled, pre_grad, act),
                [SMEM_SPEC, VMEM_SPEC, VMEM_SPEC, hidden_spec, hidden_spec],
                micros=5.5,
                deps=(dep,),
                grid=(4,),
            )
            return in_other, out_other

        if layer == last:
            in_other, out_other = other_core(term)

        upstream, gain_two, term, *weight_grads = call(
            attend_back_kernel,
            [
                ((rows, width), F32),
                ((1, width), F32),
                ((rows, width), BF16),
                *[((2 * width, local), BF16)] * 2,
            ],
            (where, term, got, mid, gains, upstream, a, proj, mixed, attn_qkv, attn_out),
            [SMEM_SPEC]
            + [VMEM_SPEC] * 3
            + [gain_spec(layer)]
            + [VMEM_SPEC] * 4
            + [layer_spec((1, 3, width, local), layer), layer_spec((1, local, width), layer)],
            [pltpu.VMEM((3, rows, local), BF16), pltpu.VMEM((rows, local), BF16)],
            micros=32,
            deps=(in_other, out_other) if layer == last else (grad_in,),
        )
        if layer < last:
            in_other, out_other = other_core(term)
        in_got, out_got = swap(in_other, "replica"), swap(out_other, "replica")
        mine, other = weight_grads
        sums[layer] = ExpertSum(mine, swap(other, "replica"), experts)
        got = swap(term, "tensor")
        in_far, out_far = call(
            grad_far_kernel,
            [
                ((half, hidden), BF16, columns((half, part))),
                ((hidden, half), BF16, lines((part, half))),
            ],
            (where, received, scaled, pre_grad, act, in_got, out_got),
            [
                SMEM_SPEC,
                VMEM_SPEC,
                VMEM_SPEC,
                columns((slots, part), 2),
                columns((slots, part), 2),
                columns((half, part), 2),
                lines((part, half), 2),
            ],
            micros=4.5,
            deps=(term,) if layer else (got,),
            grid=(2,),
        )
        if layer > 0:
            upstream, gain_one, send = call(
                functools.partial(stream_back_kernel, True),
                [((rows, width), F32), ((1, width), F32), rows_out],
                (term, got, h, gains, upstream, place),
                [VMEM_SPEC] * 3 + [gain_spec(layer), VMEM_SPEC, place_spec(layer - 1)],
                micros=2,
                deps=(in_far, out_far, sums[last].split()),
            )
            received_grad = exchange(send)
        else:
            upstream, gain_one = call(
                functools.partial(stream_back_kernel, False),
                [((row_count, width), F32), ((1, width), F32)],
                (term, got, h, gains, upstream),
                [VMEM_SPEC] * 3 + [gain_spec(layer), VMEM_SPEC],
            )
        in_far, out_far = far = swap(in_far, "tensor"), swap(out_far, "tensor")
        small.append(jnp.concatenate([gain_one, gain_two]))

        def finish_own(deps, layer=layer, args=(where, received, scaled, pre_grad, act, in_got, out_got, in_far, out_far)):
            nonlocal grad_in, grad_out
            stacked = () if grad_in is None else (grad_in, grad_out)
            grad_in, grad_out = call(
                grad_own_kernel,
                [
                    (
                        (layers, half, hidden),
                        F32,
                        pl.BlockSpec((1, half, part), lambda step: (layer, 0, step)),
                    ),
                    (
                        (layers, hidden, half),
                        F32,
                        pl.BlockSpec((1, part, half), lambda step: (layer, step, 0)),
                    ),
                ],
                (*args, *stacked),
                [
                    SMEM_SPEC,
                    VMEM_SPEC,
                    VMEM_SPEC,
                    hidden_spec,
                    hidden_spec,
                    columns((half, part)),
                    lines((part, half)),
                    columns((half, part)),
                    lines((part, half)),
                    *([ANY_SPEC] * len(stacked)),
                ],
                micros=4.5,
                deps=deps,
                grid=(2,),
                alias={9: 0, 10: 1} if stacked else None,
            )

        finishers.append(finish_own)

    finishers[1]((upstream,))

    [done] = call(
        unpack_kernel,
        [((rows, width), BF16)],
        (place, reply),
        [place_spec(last), VMEM_SPEC],
        micros=2,
        deps=(sums[0].split(),),
    )
    done = done.astype(F32) + swap(done, "tensor").astype(F32)
    mixed_out = gathered((saved[last][4] + done).astype(BF16))
    small = sum_small(jnp.concatenate([router_all, *small]))

    stacked = ()
    for layer in reversed(range(layers)):
        if layer < last:
            sums[layer].split((gain_one,))
            sums[layer].finish(far[:1])
            sums[layer].join()
            sums[layer].join((far[1], small, mixed_out))
        mine = sums[layer].result()
        stacked = call(
            layout_kernel,
            [
                ((layers, 3, width, local), F32, layer_spec((1, 3, width, local), layer)),
                ((layers, local, width), F32, layer_spec((1, local, width), layer)),
            ],
            (where, mine, swap(mine, "replica"), *stacked),
            [SMEM_SPEC, VMEM_SPEC, VMEM_SPEC] + [ANY_SPEC] * len(stacked),
            micros=2,
            alias={3: 0, 4: 1} if stacked else None,
        )
    grad_qkv, grad_proj = stacked
    router_all = small[: layers * experts].reshape(layers, experts, width)[::-1]
    small = small[layers * experts :].reshape(layers, 2, width)[::-1]
    return (
        mixed_out,
        upstream,
        small,
        grad_qkv,
        grad_proj,
        jnp.swapaxes(router_all, 1, 2),
        grad_in[:, None],
        grad_out[:, None],
    )


def solution(mesh):
    return jax.shard_map(
        on_device,
        mesh=mesh,
        in_specs=(
            P(("expert", "replica"), None),
            P(),
            P(None, None, None, "tensor"),
            P(None, "tensor", None),
            P(),
            P(None, "expert", None, "tensor"),
            P(None, "expert", "tensor", None),
            P(None, ("expert", "replica"), None),
            P(("expert", "replica"), None),
        ),
        out_specs=(
            P(("expert", "replica"), None),
            P(("expert", "replica"), None),
            P(),
            P(None, None, None, "tensor"),
            P(None, "tensor", None),
            P(),
            P(None, "expert", "replica", "tensor"),
            P(None, "expert", "tensor", "replica"),
        ),
        check_vma=False,
    )
```

```python
import functools

import jax
import jax.numpy as jnp
from jax import lax
from jax.experimental import pallas as pl
from jax.experimental.pallas import tpu as pltpu
from jax.sharding import PartitionSpec as P

HEAD_DIM = 64
SEQ = 197
PAD = 208
PAIR = 2 * HEAD_DIM
EPSILON = 1e-06
GELU_A = 0.7978845608028654
GELU_B = 0.044715
F32 = jnp.float32
BF16 = jnp.bfloat16
NT = (((1,), (1,)), ((), ()))
TN = (((0,), (0,)), ((), ()))


def mm(a, b):
    return jnp.dot(a, b, preferred_element_type=F32)


def mm_nt(a, b):
    return lax.dot_general(a, b, NT, preferred_element_type=F32)


def mm_tn(a, b):
    return lax.dot_general(a, b, TN, preferred_element_type=F32)


def normalize(stream):
    shifted = stream - jnp.mean(stream, axis=-1, keepdims=True)
    scale = lax.rsqrt(jnp.mean(shifted * shifted, axis=-1, keepdims=True) + EPSILON)
    return shifted * scale, scale


def norm_back(stream, gain, out_grad):
    xhat, scale = normalize(stream)
    u = out_grad * gain
    mean_u = jnp.mean(u, axis=-1, keepdims=True)
    mean_ux = jnp.mean(u * xhat, axis=-1, keepdims=True)
    return scale * (u - mean_u - xhat * mean_ux), jnp.sum(out_grad * xhat, axis=0, keepdims=True)


def both(own_ref, got_ref):
    return own_ref[...].astype(F32) + got_ref[...].astype(F32)


VMEM_SPEC = pl.BlockSpec(memory_space=pltpu.VMEM)
SMEM_SPEC = pl.BlockSpec(memory_space=pltpu.SMEM)
ANY_SPEC = pl.BlockSpec(memory_space=pl.ANY)


def call(body, outs, args, specs, scratch=(), micros=1.5, limit=40, deps=(), grid=(1,), alias=None):
    out_specs = [o[2] if len(o) > 2 else VMEM_SPEC for o in outs]
    outs = [jax.ShapeDtypeStruct(o[0], o[1]) for o in outs]
    taken, last = len(args), len(args) + len(deps)

    def kernel(*refs):
        body(*refs[:taken], *refs[last:])

    return pl.pallas_call(
        kernel,
        grid=grid,
        out_shape=outs,
        in_specs=[*specs, *([ANY_SPEC] * len(deps))],
        out_specs=out_specs,
        scratch_shapes=list(scratch),
        input_output_aliases=alias or {},
        compiler_params=pltpu.CompilerParams(vmem_limit_bytes=limit << 20),
        cost_estimate=pl.CostEstimate(flops=1, bytes_accessed=int(micros * 1.8e6), transcendentals=0),
    )(*args, *deps)


def layer_spec(shape, layer):
    return pl.BlockSpec(shape, lambda step: (layer,) + (0,) * (len(shape) - 1))


def place_kernel(slot_half, where_ref, routes_ref, rows_ref, place_ref, send_ref):
    layers, _, rows = routes_ref.shape
    experts = place_ref.shape[1] // slot_half
    first = where_ref[0] * slot_half
    before_of = lax.broadcasted_iota(jnp.int32, (rows, rows), 0) < lax.broadcasted_iota(
        jnp.int32, (rows, rows), 1
    )
    earlier = jnp.where(before_of, 1.0, 0.0).astype(BF16)
    labels = lax.broadcasted_iota(jnp.int32, (experts, rows), 0)
    slots = lax.broadcasted_iota(jnp.int32, (slot_half, rows), 0)
    for layer in range(layers):
        named = (labels == routes_ref[layer, 0:1, :]) | (labels == routes_ref[layer, 1:2, :])
        count = mm(jnp.where(named, 1.0, 0.0).astype(BF16), earlier)
        slot = jnp.where(named, count.astype(jnp.int32) - first, -1)
        for e in range(experts):
            hit = slots == slot[e : e + 1, :]
            place_ref[layer, e * slot_half : (e + 1) * slot_half, :] = jnp.where(
                hit, 1.0, 0.0
            ).astype(BF16)
    send_ref[...] = mm(place_ref[layers - 1], rows_ref[...]).astype(BF16)


def piece_of(matrix_in, matrix_out, layer, core):
    if matrix_in is not None:
        part = matrix_in.shape[3] // 2
        return matrix_in.at[layer, 0, :, pl.ds(pl.multiple_of(core * part, part), part)]
    part = matrix_out.shape[2] // 2
    return matrix_out.at[layer, 0, pl.ds(pl.multiple_of(core * part, part), part), :]


def fetch_kernel(layer, where_ref, source_ref, piece_ref, sem):
    copy = pltpu.make_async_copy(
        piece_of(source_ref, None, layer, where_ref[2]), piece_ref, sem.at[0]
    )
    copy.start()
    copy.wait()


def unpack_kernel(place_ref, got_ref, out_ref):
    out_ref[...] = mm_tn(place_ref[0], got_ref[...]).astype(BF16)


def unpack_pass_kernel(place_ref, got_ref, reply_ref, out_ref, passed_ref, sem):
    copy = pltpu.make_async_copy(reply_ref, passed_ref, sem.at[0])
    copy.start()
    out_ref[...] = mm_tn(place_ref[0], got_ref[...]).astype(BF16)
    copy.wait()


def pair_masks():
    lane = lax.broadcasted_iota(jnp.int32, (PAD, PAIR), 1)
    return lane < HEAD_DIM


def softmax_rows(q, k):
    scores = mm_nt(q, k) * HEAD_DIM ** (-0.5)
    column = lax.broadcasted_iota(jnp.int32, scores.shape, 1)
    scores = jnp.where(column < SEQ, scores, -1e30)
    top = jnp.max(scores, axis=-1, keepdims=True)
    weights = jnp.exp(scores - top)
    return weights / jnp.sum(weights, axis=-1, keepdims=True)


def attend_kernel(first, *refs):
    if first:
        tokens_ref, gain_ref, qkv_ref, wo_ref, h_ref, a_ref, proj_ref, mixed_ref, out_ref = refs
        h = tokens_ref[...].astype(F32)
    else:
        mid_ref, own_ref, got_ref, gain_ref, qkv_ref, wo_ref = refs[:6]
        h_ref, a_ref, proj_ref, mixed_ref, out_ref = refs[6:]
        h = mid_ref[...] + both(own_ref, got_ref)
    h_ref[...] = h
    a = (normalize(h)[0] * gain_ref[0, 0:1, :]).astype(BF16)
    a_ref[...] = a
    for c in range(3):
        proj_ref[c] = mm(a, qkv_ref[0, c]).astype(BF16)
    low = pair_masks()
    zero = jnp.zeros((PAD, PAIR), BF16)
    for image in range(a.shape[0] // PAD):
        rows = slice(image * PAD, (image + 1) * PAD)
        for pair in range(proj_ref.shape[2] // PAIR):
            lanes = slice(pair * PAIR, (pair + 1) * PAIR)
            q, k, v = (proj_ref[c, rows, lanes] for c in range(3))
            p0 = softmax_rows(jnp.where(low, q, zero), k).astype(BF16)
            p1 = softmax_rows(jnp.where(low, zero, q), k).astype(BF16)
            mixed_ref[rows, lanes] = jnp.where(low, mm(p0, v), mm(p1, v)).astype(BF16)
    out_ref[...] = mm(mixed_ref[...], wo_ref[0]).astype(BF16)


def route_kernel(
    layer, where_ref, h_ref, own_ref, got_ref, gain_ref, place_ref, source_ref, mid_ref, send_ref, piece_ref, sem
):
    copy = pltpu.make_async_copy(
        piece_of(None, source_ref, layer, where_ref[2]), piece_ref, sem.at[0]
    )
    copy.start()
    mid = h_ref[...] + both(own_ref, got_ref)
    mid_ref[...] = mid
    z = (normalize(mid)[0] * gain_ref[0, 1:2, :]).astype(BF16)
    send_ref[...] = mm(place_ref[0], z).astype(BF16)
    copy.wait()


def load_weights(layer, core, sources, win, wout, sems, in_first):
    win_own, win_a, win_b, wout_own, wout_a, wout_b = sources
    part = win.shape[2]
    groups = []
    for c in range(2):
        groups.append(
            [
                (win_own.at[layer, 0, :, pl.ds(c * part, part)], win.at[c], 2 * c),
                (wout_own.at[layer, 0, pl.ds(c * part, part), :], wout.at[c], 2 * c + 1),
            ]
        )
    groups.append(
        [
            (win_a, win.at[2 + core], 4),
            (wout_a, wout.at[2 + core], 5),
            (win_b, win.at[3 - core], 6),
            (wout_b, wout.at[3 - core], 7),
        ]
    )
    groups = [[pltpu.make_async_copy(s, d, sems.at[i]) for s, d, i in group] for group in groups]

    @pl.when(pl.program_id(0) == 0)
    def _():
        for group in groups:
            for copy in group:
                copy.start()

    for step, group in enumerate(groups):

        @pl.when(pl.program_id(0) == step)
        def _(group=group):
            for copy in group:
                copy.wait()


def gate_of(x, router, expert):
    logits = mm_nt(x, router)
    gate = jnp.exp(logits - jnp.max(logits, axis=-1, keepdims=True))
    gate = gate / jnp.sum(gate, axis=-1, keepdims=True)
    mine = lax.broadcasted_iota(jnp.int32, gate.shape, 1) == expert
    return gate, mine, jnp.sum(jnp.where(mine, gate, 0.0), axis=-1, keepdims=True)


def bend(pre):
    square = pre * pre
    bent = jnp.tanh(pre * (GELU_A + (GELU_A * GELU_B) * square))
    half = 0.5 + 0.5 * bent
    slope = half + pre * (1.0 - bent * bent) * (0.5 * GELU_A + (1.5 * GELU_A * GELU_B) * square)
    return pre * half, slope


def add_step(total, term):
    @pl.when(pl.program_id(0) == 0)
    def _():
        total[...] = term

    @pl.when(pl.program_id(0) > 0)
    def _():
        total[...] += term


def expert_kernel(
    layer, where_ref, x_ref, router_ref, win_own, win_a, win_b, wout_own, wout_a, wout_b,
    out_ref, act_ref, slope_ref, win, wout, total, sems,
):
    step = pl.program_id(0)
    sources = (win_own, win_a, win_b, wout_own, wout_a, wout_b)
    load_weights(layer, where_ref[2], sources, win, wout, sems, True)
    act, slope = bend(mm(x_ref[...], win[step]))
    act = act.astype(BF16)
    act_ref[...] = act
    slope_ref[...] = slope.astype(BF16)
    add_step(total, mm(act, wout[step]))

    @pl.when(step == pl.num_programs(0) - 1)
    def _():
        _, _, share = gate_of(x_ref[...], router_ref[...], where_ref[1])
        out_ref[...] = (share * total[...]).astype(BF16)


def finish_back(x_ref, router_ref, gate, mine, share, dot, total, out_ref, router_grad_ref):
    logit_grad = (dot * share * (jnp.where(mine, 1.0, 0.0) - gate)).astype(BF16)
    router_grad_ref[...] = mm_tn(logit_grad, x_ref[...])
    out_ref[...] = (total + mm(logit_grad, router_ref[...])).astype(BF16)


def expert_back_kernel(
    layer, where_ref, g_ref, x_ref, act_ref, slope_ref, router_ref,
    win_own, win_a, win_b, wout_own, wout_a, wout_b,
    out_ref, pre_grad_ref, scaled_ref, router_grad_ref, win, wout, total, dot_ref, sems,
):
    step = pl.program_id(0)
    sources = (win_own, win_a, win_b, wout_own, wout_a, wout_b)
    load_weights(layer, where_ref[2], sources, win, wout, sems, False)
    g = g_ref[...]
    gate, mine, share = gate_of(x_ref[...], router_ref[...], where_ref[1])
    u = mm_nt(g, wout[step])
    pre_grad = (share * u * slope_ref[...].astype(F32)).astype(BF16)
    pre_grad_ref[...] = pre_grad
    add_step(total, mm_nt(pre_grad, win[step]))
    add_step(dot_ref, jnp.sum(u * act_ref[...].astype(F32), axis=-1, keepdims=True))

    @pl.when(step == pl.num_programs(0) - 1)
    def _():
        scaled_ref[...] = (share * g.astype(F32)).astype(BF16)
        finish_back(
            x_ref, router_ref, gate, mine, share, dot_ref[...], total[...], out_ref, router_grad_ref
        )


def expert_both_kernel(
    layer, where_ref, g_ref, x_ref, router_ref,
    win_own, win_a, win_b, wout_own, wout_a, wout_b,
    out_ref, back_ref, act_ref, pre_grad_ref, scaled_ref, router_grad_ref,
    win, wout, total, back_total, dot_ref, sems,
):
    step = pl.program_id(0)
    sources = (win_own, win_a, win_b, wout_own, wout_a, wout_b)
    load_weights(layer, where_ref[2], sources, win, wout, sems, True)
    g = g_ref[...]
    gate, mine, share = gate_of(x_ref[...], router_ref[...], where_ref[1])
    act, slope = bend(mm(x_ref[...], win[step]))
    u = mm_nt(g, wout[step])
    act = act.astype(BF16)
    act_ref[...] = act
    pre_grad = (share * u * slope).astype(BF16)
    pre_grad_ref[...] = pre_grad
    add_step(total, mm(act, wout[step]))
    add_step(back_total, mm_nt(pre_grad, win[step]))
    add_step(dot_ref, jnp.sum(u * act.astype(F32), axis=-1, keepdims=True))

    @pl.when(step == pl.num_programs(0) - 1)
    def _():
        out_ref[...] = (share * total[...]).astype(BF16)
        scaled_ref[...] = (share * g.astype(F32)).astype(BF16)
        finish_back(
            x_ref, router_ref, gate, mine, share, dot_ref[...], back_total[...], back_ref, router_grad_ref
        )


def half_of(ref, which):
    half = ref.shape[1] // 2
    return ref[:, pl.ds(pl.multiple_of(which * half, half), half)]


def grad_other_kernel(where_ref, x_ref, scaled_ref, pre_grad_ref, act_ref, in_ref, out_ref):
    other = 1 - where_ref[2]
    in_ref[...] = mm_tn(half_of(x_ref, other), pre_grad_ref[...]).astype(BF16)
    out_ref[...] = mm_tn(act_ref[...], half_of(scaled_ref, other)).astype(BF16)


def grad_far_kernel(
    where_ref, x_ref, scaled_ref, pre_grad_ref, act_ref, in_got_ref, out_got_ref, in_ref, out_ref
):
    core = where_ref[2]
    term = mm_tn(half_of(x_ref, core), pre_grad_ref[...])
    in_ref[...] = (term + in_got_ref[...].astype(F32)).astype(BF16)
    term = mm_tn(act_ref[...], half_of(scaled_ref, core))
    out_ref[...] = (term + out_got_ref[...].astype(F32)).astype(BF16)


def grad_own_kernel(
    where_ref, x_ref, scaled_ref, pre_grad_ref, act_ref, in_got_ref, out_got_ref, in_far_ref, out_far_ref, *refs
):
    core = where_ref[2]
    in_ref, out_ref = refs[-2:]
    term = mm_tn(half_of(x_ref, core), pre_grad_ref[...])
    in_ref[0] = term + in_got_ref[...].astype(F32) + in_far_ref[...].astype(F32)
    term = mm_tn(act_ref[...], half_of(scaled_ref, core))
    out_ref[0] = term + out_got_ref[...].astype(F32) + out_far_ref[...].astype(F32)


def attend_back_kernel(
    where_ref, own_ref, got_ref, mid_ref, gain_ref, g_ref, a_ref, proj_ref, mixed_ref, qkv_ref, wo_ref,
    g_out_ref, gain_grad_ref, out_ref, *refs,
):
    back_ref, mixed_grad_ref = refs[-2:]
    h_grad, gain_grad_ref[...] = norm_back(
        mid_ref[...], gain_ref[0, 1:2, :], both(own_ref, got_ref)
    )
    g = g_ref[...].astype(F32) + h_grad
    g_out_ref[...] = g
    out_grad = g.astype(BF16)
    width = proj_ref.shape[2]
    depth = a_ref.shape[1]
    mixed_grad_ref[...] = mm_nt(out_grad, wo_ref[0]).astype(BF16)
    low = pair_masks()
    zero = jnp.zeros((PAD, PAIR), BF16)
    for image in range(g.shape[0] // PAD):
        rows = slice(image * PAD, (image + 1) * PAD)
        for pair in range(width // PAIR):
            lanes = slice(pair * PAIR, (pair + 1) * PAIR)
            q, k, v = (proj_ref[c, rows, lanes] for c in range(3))
            dm = mixed_grad_ref[rows, lanes]
            parts = []
            for side in range(2):
                def pick(t, side=side):
                    return jnp.where(low, t, zero) if side == 0 else jnp.where(low, zero, t)

                probs = softmax_rows(pick(q), k)
                prob_grad = mm_nt(pick(dm), v)
                row = jnp.sum(prob_grad * probs, axis=-1, keepdims=True)
                score_grad = (probs * (prob_grad - row)).astype(BF16)
                parts.append(
                    (
                        mm(score_grad, k) * HEAD_DIM ** (-0.5),
                        mm_tn(score_grad, q) * HEAD_DIM ** (-0.5),
                        mm_tn(probs.astype(BF16), dm),
                    )
                )
            for c in range(3):
                back_ref[c, rows, lanes] = jnp.where(low, parts[0][c], parts[1][c]).astype(BF16)
    total = mm_nt(back_ref[0], qkv_ref[0, 0])
    total += mm_nt(back_ref[1], qkv_ref[0, 1])
    total += mm_nt(back_ref[2], qkv_ref[0, 2])
    out_ref[...] = total.astype(BF16)
    core = where_ref[2]

    def put(block, start, value):
        @pl.when(core == block // 2)
        def _():
            refs[0][start : start + value.shape[0], :] = value.astype(BF16)

        @pl.when(core != block // 2)
        def _():
            refs[1][start : start + value.shape[0], :] = value.astype(BF16)

    for c in range(3):
        put(c, c % 2 * depth, mm_tn(a_ref[...], back_ref[c]))
    proj_grad = mm_tn(mixed_ref[...], out_grad)
    for c in range(depth // width):
        put(3, depth + c * width, proj_grad[:, c * width : (c + 1) * width])


def stream_back_kernel(pack, *refs):
    if pack:
        own_ref, got_ref, h_ref, gain_ref, g_ref, place_ref, g_out_ref, gain_grad_ref, send_ref = refs
    else:
        own_ref, got_ref, h_ref, gain_ref, g_ref, g_out_ref, gain_grad_ref = refs
    h_grad, gain_grad_ref[...] = norm_back(h_ref[...], gain_ref[0, 0:1, :], both(own_ref, got_ref))
    g = g_ref[...] + h_grad
    if not pack:
        for image in range(g.shape[0] // PAD):
            g_out_ref[image * SEQ : (image + 1) * SEQ, :] = g[image * PAD : image * PAD + SEQ, :]
    if pack:
        g_out_ref[...] = g
        send_ref[...] = mm(place_ref[0], g.astype(BF16)).astype(BF16)


def swap(value, axis):
    return lax.ppermute(value, axis, [(0, 1), (1, 0)])


def partner(value, axis, bit):
    count = lax.axis_size(axis)
    return lax.ppermute(value, axis, [(i, i ^ (1 << bit)) for i in range(count)])


def first_split_kernel(sides_ref, mine_ref, got_ref, *outs):
    for i in range(2):
        out_ref, send_ref = outs[2 * i], outs[2 * i + 1]
        half = out_ref.shape[0]
        side = sides_ref[i]
        mine, other = pl.ds(side * half, half), pl.ds((1 - side) * half, half)
        out_ref[...] = mine_ref[i, mine].astype(F32) + got_ref[i, mine].astype(F32)
        send_ref[...] = (mine_ref[i, other].astype(F32) + got_ref[i, other].astype(F32)).astype(BF16)


def last_join_kernel(sides_ref, own_a_ref, got_a_ref, own_b_ref, got_b_ref, out_ref):
    for i, (own_ref, got_ref) in enumerate(((own_a_ref, got_a_ref), (own_b_ref, got_b_ref))):
        half = own_ref.shape[0]
        side = sides_ref[i]
        out_ref[i, pl.ds(side * half, half)] = own_ref[...]
        out_ref[i, pl.ds((1 - side) * half, half)] = got_ref[...]


def layout_kernel(where_ref, mine_ref, got_ref, *refs):
    qkv_ref, proj_ref = refs[-2:]
    depth, width = qkv_ref.shape[2:]

    def write(low_ref, high_ref):
        qkv_ref[0, 0] = low_ref[0].astype(F32)
        qkv_ref[0, 1] = low_ref[1].astype(F32)
        qkv_ref[0, 2] = high_ref[0].astype(F32)
        for c in range(depth // width):
            rows = slice(c * width, (c + 1) * width)
            proj_ref[0, :, rows] = high_ref[1, rows, :].astype(F32)

    @pl.when(where_ref[2] == 0)
    def _():
        write(mine_ref, got_ref)

    @pl.when(where_ref[2] == 1)
    def _():
        write(got_ref, mine_ref)


def split_kernel(sides_ref, keep_a_ref, got_a_ref, keep_b_ref, got_b_ref, *outs):
    for i, (keep_ref, got_ref) in enumerate(((keep_a_ref, got_a_ref), (keep_b_ref, got_b_ref))):
        out_ref, send_ref = outs[2 * i], outs[2 * i + 1]
        half = out_ref.shape[0]
        side = sides_ref[i]
        mine, other = pl.ds(side * half, half), pl.ds((1 - side) * half, half)
        out_ref[...] = keep_ref[mine].astype(F32) + got_ref[mine].astype(F32)
        send_ref[...] = (keep_ref[other].astype(F32) + got_ref[other].astype(F32)).astype(BF16)


def last_sum_kernel(keep_a_ref, got_a_ref, keep_b_ref, got_b_ref, a_ref, b_ref):
    a_ref[...] = both(keep_a_ref, got_a_ref).astype(BF16)
    b_ref[...] = both(keep_b_ref, got_b_ref).astype(BF16)


def join_kernel(sides_ref, own_a_ref, got_a_ref, own_b_ref, got_b_ref, a_ref, b_ref):
    pairs = ((own_a_ref, got_a_ref, a_ref), (own_b_ref, got_b_ref, b_ref))
    for i, (own_ref, got_ref, out_ref) in enumerate(pairs):
        half = own_ref.shape[0]
        side = sides_ref[i]
        out_ref[pl.ds(side * half, half)] = own_ref[...]
        out_ref[pl.ds((1 - side) * half, half)] = got_ref[...]


class ExpertSum:
    def __init__(self, mine, got, experts):
        rows, width = mine.shape
        block = rows // (2 * experts)
        mine, got = (v.reshape(2, experts, block, width) for v in (mine, got))
        bits = list(range(experts.bit_length() - 1))
        self.orders = list(zip(bits, [*bits[1::-1], *bits[2:]]))
        me = lax.axis_index("expert")
        self.sides = [jnp.stack([(me >> a) & 1, (me >> b) & 1]).astype(jnp.int32) for a, b in self.orders]
        self.state = (mine, got)
        self.count, self.block, self.width = experts, block, width
        self.step = 0

    def shape(self):
        return (self.count, self.block, self.width)

    def split(self, deps=()):
        self.count //= 2
        a, b = self.orders[self.step]
        keep_a, send_a, keep_b, send_b = call(
            first_split_kernel if self.step == 0 else split_kernel,
            [(self.shape(), F32), (self.shape(), BF16)] * 2,
            (self.sides[self.step], *self.state),
            [SMEM_SPEC] + [VMEM_SPEC] * len(self.state),
            deps=deps,
        )
        self.step += 1
        self.state = (keep_a, partner(send_a, "expert", a), keep_b, partner(send_b, "expert", b))
        return send_a

    def finish(self, deps=()):
        while self.step < len(self.orders):
            self.split()
        self.state = call(
            last_sum_kernel, [(self.shape(), BF16)] * 2, self.state, [VMEM_SPEC] * 4, deps=deps
        )
        return self.state[0]

    def join(self, deps=()):
        self.step -= 1
        own_a, own_b = self.state
        a, b = self.orders[self.step]
        got_a, got_b = partner(own_a, "expert", a), partner(own_b, "expert", b)
        self.count *= 2
        self.state = call(
            join_kernel if self.step else last_join_kernel,
            [(self.shape(), BF16)] * 2 if self.step else [((2, *self.shape()), BF16)],
            (self.sides[self.step], own_a, got_a, own_b, got_b),
            [SMEM_SPEC] + [VMEM_SPEC] * 4,
            deps=deps,
        )
        return self.state[0]

    def result(self):
        while self.step:
            self.join()
        return self.state[0].reshape(2, -1, self.width)


def sum_small(value):
    value = value + swap(value, "replica")
    for bit in range(lax.axis_size("expert").bit_length() - 1):
        value = value + partner(value, "expert", bit)
    return value


def on_device(tokens, gains, attn_qkv, attn_out, router, expert_in, expert_out, routes, cotangent):
    row_count, width = tokens.shape
    layers = attn_qkv.shape[0]
    local = attn_qkv.shape[3]
    images = row_count // SEQ
    rows = images * PAD
    experts = router.shape[2]
    hidden = expert_in.shape[3]
    part = hidden // 2
    half = width // 2
    capacity = 8 * (5 * row_count // (16 * experts) + 1)
    slot_half = capacity // 2
    slots = experts * slot_half
    side = lax.axis_index("tensor")
    core = lax.axis_index("replica")
    where = jnp.stack([side, lax.axis_index("expert"), core]).astype(jnp.int32)
    last = layers - 1

    def spread(array):
        array = array.reshape(images, SEQ, width)
        return jnp.pad(array, ((0, 0), (0, PAD - SEQ), (0, 0))).reshape(rows, width)

    def gathered(array):
        return array.reshape(images, PAD, width)[:, :SEQ].reshape(row_count, width)

    def exchange(block):
        block = block.reshape(experts, slot_half, width)
        return lax.all_to_all(block, "expert", 0, 0, tiled=True).reshape(slots, width)

    def fetch(layer, deps=()):
        [piece] = call(
            functools.partial(fetch_kernel, layer),
            [((width, part), BF16, ANY_SPEC)],
            (where, expert_in),
            [SMEM_SPEC, ANY_SPEC],
            [pltpu.SemaphoreType.DMA((1,))],
            deps=deps,
        )
        return piece, pair_of(piece)

    def pair_of(piece):
        got = swap(piece, "tensor")
        return got, swap(got, "replica")

    def place_spec(layer):
        return layer_spec((1, slots, rows), layer)

    def gain_spec(layer):
        return layer_spec((1, 2, width), layer)

    def columns(size, shift=0):
        return pl.BlockSpec(size, lambda step: (0, step + shift))

    def lines(size, shift=0):
        return pl.BlockSpec(size, lambda step: (step + shift, 0))

    weights = [pltpu.VMEM((4, width, part), BF16), pltpu.VMEM((4, part, width), BF16)]
    total = pltpu.VMEM((slots, width), F32)
    dots = pltpu.VMEM((slots, 1), F32)
    sems = pltpu.SemaphoreType.DMA((8,))
    rows_out = ((slots, width), BF16)
    hidden_spec = columns((slots, part))
    hidden_out = ((slots, 2 * hidden), BF16, hidden_spec)

    _, whole_in = fetch(0)
    attend_deps = ()
    router_t = jnp.swapaxes(router, 1, 2)
    routes_t = jnp.swapaxes(routes, 1, 2).reshape(layers, 2, images, SEQ)
    routes_t = jnp.pad(
        routes_t, ((0, 0), (0, 0), (0, 0), (0, PAD - SEQ)), constant_values=-1
    ).reshape(layers, 2, rows)
    upstream = spread(cotangent)
    stream_args = (spread(tokens),)
    place = None
    saved = []
    for layer in range(layers):
        h, a, proj, mixed, term = call(
            functools.partial(attend_kernel, layer == 0),
            [
                ((rows, width), F32),
                ((rows, width), BF16),
                ((3, rows, local), BF16),
                ((rows, local), BF16),
                ((rows, width), BF16),
            ],
            (*stream_args, gains, attn_qkv, attn_out),
            [
                *([VMEM_SPEC] * len(stream_args)),
                gain_spec(layer),
                layer_spec((1, 3, width, local), layer),
                layer_spec((1, local, width), layer),
            ],
            micros=5,
            deps=attend_deps,
        )
        if place is None:
            place, send = call(
                functools.partial(place_kernel, slot_half),
                [((layers, slots, rows), BF16), rows_out],
                (where, routes_t, upstream),
                [SMEM_SPEC, VMEM_SPEC, VMEM_SPEC],
                micros=1.5,
                deps=(term,),
            )
            received_grad = exchange(send)
        mid, send, piece = call(
            functools.partial(route_kernel, layer),
            [((rows, width), F32), rows_out, ((part, width), BF16, ANY_SPEC)],
            (where, h, term, swap(term, "tensor"), gains, place, expert_out),
            [SMEM_SPEC] + [VMEM_SPEC] * 3 + [gain_spec(layer), place_spec(layer), ANY_SPEC],
            [pltpu.SemaphoreType.DMA((1,))],
            micros=2,
        )
        whole = (expert_in, *whole_in, expert_out, *pair_of(piece))
        received = exchange(send)
        if layer < last:
            piece, whole_in = fetch(layer + 1, (received,))
            attend_deps = (whole_in[0],)
            reply, act, slope = call(
                functools.partial(expert_kernel, layer),
                [rows_out, hidden_out, hidden_out],
                (where, received, router_t[layer], *whole),
                [SMEM_SPEC, VMEM_SPEC, VMEM_SPEC] + [ANY_SPEC] * 6,
                [*weights, total, sems],
                micros=13,
                limit=56,
                deps=(piece,),
                grid=(4,),
            )
            returned = exchange(reply)
            [term] = call(
                unpack_kernel,
                [((rows, width), BF16)],
                (place, returned),
                [place_spec(layer), VMEM_SPEC],
                micros=2,
            )
            stream_args = (mid, term, swap(term, "tensor"))
            saved.append((h, a, proj, mixed, mid, received, act, slope, whole))
        else:
            saved.append((h, a, proj, mixed, mid, received, None, None, whole))

    small, router_grads = [], []
    sums = [None] * layers
    grad_in = grad_out = None
    finishers = []
    for layer in reversed(range(layers)):
        h, a, proj, mixed, mid, received, act, slope, whole = saved[layer]
        back_outs = [hidden_out, rows_out, ((experts, width), F32)]
        if layer == last:
            reply, back, act, pre_grad, scaled, router_grad = call(
                functools.partial(expert_both_kernel, layer),
                [rows_out, rows_out, hidden_out, *back_outs],
                (where, received_grad, received, router_t[layer], *whole),
                [SMEM_SPEC] + [VMEM_SPEC] * 3 + [ANY_SPEC] * 6,
                [*weights, total, total, dots, sems],
                micros=22,
                limit=56,
                grid=(4,),
            )
        else:
            back, pre_grad, scaled, router_grad = call(
                functools.partial(expert_back_kernel, layer),
                [rows_out, *back_outs],
                (where, received_grad, received, act, slope, router_t[layer], *whole),
                [SMEM_SPEC, VMEM_SPEC, VMEM_SPEC, hidden_spec, hidden_spec, VMEM_SPEC] + [ANY_SPEC] * 6,
                [*weights, total, dots, sems],
                micros=13,
                limit=56,
                deps=(far[0], sums[last].split()),
                grid=(4,),
            )
        returned = exchange(back)
        router_grads.append(router_grad)
        if layer == 0:
            router_all = jnp.concatenate(router_grads)
            router_all = router_all + swap(router_all, "tensor")
        if layer == last:
            term, reply = call(
                unpack_pass_kernel,
                [((rows, width), BF16), (*rows_out, ANY_SPEC)],
                (place, returned, reply),
                [place_spec(layer), VMEM_SPEC, ANY_SPEC],
                [pltpu.SemaphoreType.DMA((1,))],
                micros=2,
            )
        else:
            [term] = call(
                unpack_kernel,
                [((rows, width), BF16)],
                (place, returned),
                [place_spec(layer), VMEM_SPEC],
                micros=2,
                deps=(far[1], sums[last].finish(), router_all),
            )
            finishers[0]((term,))
            reply = exchange(reply)
        got = swap(term, "tensor")
        def other_core(dep):
            in_other, out_other = call(
                grad_other_kernel,
                [
                    ((half, 2 * hidden), BF16, columns((half, part))),
                    ((2 * hidden, half), BF16, lines((part, half))),
                ],
                (where, received, scaled, pre_grad, act),
                [SMEM_SPEC, VMEM_SPEC, VMEM_SPEC, hidden_spec, hidden_spec],
                micros=5.5,
                deps=(dep,),
                grid=(4,),
            )
            return in_other, out_other

        if layer == last:
            in_other, out_other = other_core(term)

        upstream, gain_two, term, *weight_grads = call(
            attend_back_kernel,
            [
                ((rows, width), F32),
                ((1, width), F32),
                ((rows, width), BF16),
                *[((2 * width, local), BF16)] * 2,
            ],
            (where, term, got, mid, gains, upstream, a, proj, mixed, attn_qkv, attn_out),
            [SMEM_SPEC]
            + [VMEM_SPEC] * 3
            + [gain_spec(layer)]
            + [VMEM_SPEC] * 4
            + [layer_spec((1, 3, width, local), layer), layer_spec((1, local, width), layer)],
            [pltpu.VMEM((3, rows, local), BF16), pltpu.VMEM((rows, local), BF16)],
            micros=32,
            deps=(in_other, out_other) if layer == last else (grad_in,),
        )
        if layer < last:
            in_other, out_other = other_core(term)
        in_got, out_got = swap(in_other, "replica"), swap(out_other, "replica")
        mine, other = weight_grads
        sums[layer] = ExpertSum(mine, swap(other, "replica"), experts)
        got = swap(term, "tensor")
        in_far, out_far = call(
            grad_far_kernel,
            [
                ((half, hidden), BF16, columns((half, part))),
                ((hidden, half), BF16, lines((part, half))),
            ],
            (where, received, scaled, pre_grad, act, in_got, out_got),
            [
                SMEM_SPEC,
                VMEM_SPEC,
                VMEM_SPEC,
                columns((slots, part), 2),
                columns((slots, part), 2),
                columns((half, part), 2),
                lines((part, half), 2),
            ],
            micros=4.5,
            deps=(term,) if layer else (got,),
            grid=(2,),
        )
        if layer > 0:
            upstream, gain_one, send = call(
                functools.partial(stream_back_kernel, True),
                [((rows, width), F32), ((1, width), F32), rows_out],
                (term, got, h, gains, upstream, place),
                [VMEM_SPEC] * 3 + [gain_spec(layer), VMEM_SPEC, place_spec(layer - 1)],
                micros=2,
                deps=(in_far, out_far, sums[last].split()),
            )
            received_grad = exchange(send)
        else:
            upstream, gain_one = call(
                functools.partial(stream_back_kernel, False),
                [((row_count, width), F32), ((1, width), F32)],
                (term, got, h, gains, upstream),
                [VMEM_SPEC] * 3 + [gain_spec(layer), VMEM_SPEC],
            )
        in_far, out_far = far = swap(in_far, "tensor"), swap(out_far, "tensor")
        small.append(jnp.concatenate([gain_one, gain_two]))

        def finish_own(deps, layer=layer, args=(where, received, scaled, pre_grad, act, in_got, out_got, in_far, out_far)):
            nonlocal grad_in, grad_out
            stacked = () if grad_in is None else (grad_in, grad_out)
            grad_in, grad_out = call(
                grad_own_kernel,
                [
                    (
                        (layers, half, hidden),
                        F32,
                        pl.BlockSpec((1, half, part), lambda step: (layer, 0, step)),
                    ),
                    (
                        (layers, hidden, half),
                        F32,
                        pl.BlockSpec((1, part, half), lambda step: (layer, step, 0)),
                    ),
                ],
                (*args, *stacked),
                [
                    SMEM_SPEC,
                    VMEM_SPEC,
                    VMEM_SPEC,
                    hidden_spec,
                    hidden_spec,
                    columns((half, part)),
                    lines((part, half)),
                    columns((half, part)),
                    lines((part, half)),
                    *([ANY_SPEC] * len(stacked)),
                ],
                micros=4.5,
                deps=deps,
                grid=(2,),
                alias={9: 0, 10: 1} if stacked else None,
            )

        finishers.append(finish_own)

    finishers[1]((upstream,))

    [done] = call(
        unpack_kernel,
        [((rows, width), BF16)],
        (place, reply),
        [place_spec(last), VMEM_SPEC],
        micros=2,
        deps=(sums[0].split(),),
    )
    done = done.astype(F32) + swap(done, "tensor").astype(F32)
    mixed_out = gathered((saved[last][4] + done).astype(BF16))
    small = sum_small(jnp.concatenate([router_all, *small]))

    stacked = ()
    for layer in reversed(range(layers)):
        if layer < last:
            sums[layer].split((gain_one,))
            sums[layer].finish(far[:1])
            sums[layer].join()
            sums[layer].join((far[1],))
            while sums[layer].step:
                sums[layer].join((small, mixed_out) if sums[layer].step == 1 else ())
        mine = sums[layer].result()
        stacked = call(
            layout_kernel,
            [
                ((layers, 3, width, local), F32, layer_spec((1, 3, width, local), layer)),
                ((layers, local, width), F32, layer_spec((1, local, width), layer)),
            ],
            (where, mine, swap(mine, "replica"), *stacked),
            [SMEM_SPEC, VMEM_SPEC, VMEM_SPEC] + [ANY_SPEC] * len(stacked),
            micros=2,
            alias={3: 0, 4: 1} if stacked else None,
        )
    grad_qkv, grad_proj = stacked
    router_all = small[: layers * experts].reshape(layers, experts, width)[::-1]
    small = small[layers * experts :].reshape(layers, 2, width)[::-1]
    return (
        mixed_out,
        upstream,
        small,
        grad_qkv,
        grad_proj,
        jnp.swapaxes(router_all, 1, 2),
        grad_in[:, None],
        grad_out[:, None],
    )


def solution(mesh):
    return jax.shard_map(
        on_device,
        mesh=mesh,
        in_specs=(
            P(("expert", "replica"), None),
            P(),
            P(None, None, None, "tensor"),
            P(None, "tensor", None),
            P(),
            P(None, "expert", None, "tensor"),
            P(None, "expert", "tensor", None),
            P(None, ("expert", "replica"), None),
            P(("expert", "replica"), None),
        ),
        out_specs=(
            P(("expert", "replica"), None),
            P(("expert", "replica"), None),
            P(),
            P(None, None, None, "tensor"),
            P(None, "tensor", None),
            P(),
            P(None, "expert", "replica", "tensor"),
            P(None, "expert", "tensor", "replica"),
        ),
        check_vma=False,
    )
```
